128 devices in a mesh: tm: 16 (over x, y), tile: 8 (over z, core).
Axes of the slice: x: 4, y: 4, z: 4, core: 2. Of those that a mesh axis runs over, the one named last changes fastest.
Arguments:
- observed: float32 [9, 64, 8192], P(None, 'tile', 'tm'), may hold values from -6 to 6
- increments: float32 [9, 64, 8192], P(None, 'tile', 'tm'), may hold values from -0.15625 to 0.15625
- model: float32 [512, 256], P(('tm', 'tile')), may hold values from -6 to 6
- kernel: bfloat16 [256, 4, 9, 256, 256], P(('tm', 'tile')), may hold values from -0.1875 to 0.1875
- tile_index: int32 [256, 4], P(('tm', 'tile')), may hold values from 0 to 511, all different within a row
- station_of: int32 [64, 8192], P('tile', 'tm'), may hold values from 0 to 65535, as said below
- line_length: int32 [64], P('tile'), may hold values from 2048 to 8192, as said below
Outputs:
- grad_model: float32 [512, 256], P(('tm', 'tile'))
- grad_increments: float32 [9, 64, 8192], P(None, 'tile', 'tm')
The draws below stay inside these ranges and needn't reach their ends.
Inputs may be any that keep to these rules, and one draw needn't show every extreme that they name: `station_of`: in the samples of one index pair of tile and tm (its block of lines and block of time), no station tile (value // 256) holds more than 32 samples, and one holds exactly 32. `line_length`: some line has all 8192 samples. `tile_index`: each row names 4 different cell tiles, and every cell tile is named by some row.
All inputs are finite; a program needn't handle non-finite values.
Results may differ from the reference program's by a relative error of at most 0.0031.
Values may be sent and summed in bfloat16 or wider, within the bound.
A program may use at most 128 MiB of HBM per device.

```python
import math
import jax
import jax.numpy as jnp
from jax import lax

COMPS = 9
TILE_W = 256
NNZ = 4
LINES_DEV = 8
TIME_DEV = 512
LINES = 64
TIME = 8192
STATION_TILES = 256
CELL_TILES = 512
CAP = 32


def draw_station_of(key, part):
    block_rows = LINES_DEV * TIME_DEV
    tile_groups = LINES // LINES_DEV
    time_groups = TIME // TIME_DEV
    slot_count = STATION_TILES * CAP
    block_keys = jax.random.split(key, tile_groups * time_groups)

    def one_block(block_key):
        key_full, key_score, key_shuffle, key_inner = jax.random.split(block_key, 4)
        full_tile = jax.random.randint(key_full, (), 0, STATION_TILES)
        scores = jax.random.permutation(key_score, slot_count).astype(jnp.int32)
        slot_tile = jnp.arange(slot_count, dtype=jnp.int32) // CAP
        scores = jnp.where(slot_tile == full_tile, scores - slot_count, scores)
        chosen = jnp.argsort(scores)[:block_rows].astype(jnp.int32)
        tile_ids = jax.random.permutation(key_shuffle, chosen // CAP)
        inner_station = jax.random.randint(key_inner, (block_rows,), 0, TILE_W)
        return (tile_ids * TILE_W + inner_station).astype(jnp.int32)
    blocks = jax.vmap(one_block)(block_keys)
    shaped = blocks.reshape(tile_groups, time_groups, LINES_DEV, TIME_DEV)
    return jnp.transpose(shaped, (0, 2, 1, 3)).reshape(LINES, TIME)


def draw_line_length(key, part):
    key_length, key_pick = jax.random.split(key, 2)
    lengths = jax.random.randint(key_length, (LINES,), TIME // 4, TIME + 1)
    longest = jax.random.randint(key_pick, (), 0, LINES)
    return jnp.where(jnp.arange(LINES) == longest, TIME, lengths).astype(jnp.int32)


def level_of(own_key, extent, pieces, least, high):
    def one(position, blocks):
        heights = jax.random.uniform(jax.random.fold_in(jax.random.fold_in(own_key, 6), position), (blocks,), jnp.float32, least / len(pieces), high / len(pieces))
        return jnp.repeat(jnp.exp(heights), extent[position] // blocks).reshape((-1,) + (1,) * (len(extent) - position - 1))

    level = one(*pieces[0])
    for cut in pieces[1:]:
        level = level * one(*cut)
    return level


def picks_of(stream_key, rows, amount, top, lift):
    sequence = jax.random.permutation(jax.random.fold_in(stream_key, 1), amount)
    favour = sequence
    for power in range(3):
        favour = favour * favour // amount
    favour = favour * lift // amount
    tickets = jax.random.randint(jax.random.fold_in(stream_key, 2), (rows, amount), 0, 4096) + favour
    fixed_rows = jax.random.permutation(jax.random.fold_in(stream_key, 3), rows)[jnp.arange(amount) % rows]
    tickets = jnp.where(jnp.arange(rows)[:, None] == fixed_rows[None, :], 1 << 14, tickets)
    merit = tickets * amount + jnp.arange(amount)
    return lax.top_k(merit.astype(jnp.int32), top)[1].astype(jnp.int32)


def centred(own_key, dims, scale, reach, pieces=(), kind=jnp.bfloat16):
    drawn = scale * jax.random.normal(own_key, dims, jnp.float32)
    if pieces:
        drawn = drawn * level_of(own_key, dims, pieces, -0.22, 0.18)
    return jnp.clip(drawn, -reach, reach).astype(kind)


def setup_inputs(seed: int = 0) -> dict:
    seeds = jax.random.split(jax.random.key(seed), 8)
    return {
        "observed": centred(seeds[0], (COMPS, LINES, TIME), 1.0, 6.0, ((1, 8), (2, 16)), jnp.float32),
        "increments": centred(seeds[1], (COMPS, LINES, TIME), (TIME ** -0.5), 0.15625, ((1, 8), (2, 16)), jnp.float32),
        "model": centred(seeds[2], (CELL_TILES, TILE_W), 1.0, 6.0, ((0, 128),), jnp.float32),
        "kernel": centred(seeds[3], (STATION_TILES, NNZ, COMPS, TILE_W, TILE_W), (NNZ * TILE_W) ** -0.5, 0.1875, ((0, 128),)),
        "tile_index": picks_of(seeds[4], STATION_TILES, CELL_TILES, NNZ, 64),
        "station_of": draw_station_of(jax.random.fold_in(seeds[7], 71), 0),
        "line_length": draw_line_length(jax.random.fold_in(seeds[7], 71), 0),
    }


def reference(observed, increments, model, kernel, tile_index, station_of, line_length):
    drift_walk = jnp.cumsum(increments, axis=2)
    positions = jnp.arange(TIME, dtype=jnp.int32)
    inside = (positions[None, :] < line_length[:, None]).astype(jnp.float32)
    model_half = model.astype(jnp.bfloat16)

    def forward_tile(operands):
        blocks, chosen = operands
        cells = model_half[chosen].astype(jnp.float32)
        return jnp.einsum('kcij,kj->ci', blocks.astype(jnp.float32), cells, precision=lax.Precision.HIGHEST)
    predicted = lax.map(forward_tile, (kernel, tile_index))
    table = jnp.transpose(predicted, (1, 0, 2)).reshape(COMPS, STATION_TILES * TILE_W)
    at_sample = table[:, station_of]
    residual = inside[None] * (at_sample + drift_walk - observed)
    flat_residual = residual.reshape(COMPS, LINES * TIME)
    summed = jax.ops.segment_sum(flat_residual.T, station_of.reshape(-1), num_segments=STATION_TILES * TILE_W)
    station_gain = 1.0 / math.sqrt(LINES * TIME / (STATION_TILES * TILE_W))
    station_sums = jnp.transpose(summed.reshape(STATION_TILES, TILE_W, COMPS), (0, 2, 1))
    station_half = (station_sums * station_gain).astype(jnp.bfloat16)

    def adjoint_tile(operands):
        blocks, sums_half = operands
        return jnp.einsum('kcij,ci->kj', blocks.astype(jnp.float32), sums_half.astype(jnp.float32), precision=lax.Precision.HIGHEST)
    contributions = lax.map(adjoint_tile, (kernel, station_half))
    grad_model = jnp.zeros((CELL_TILES, TILE_W), jnp.float32).at[tile_index.reshape(-1)].add(contributions.reshape(-1, TILE_W))
    suffix = jnp.flip(jnp.cumsum(jnp.flip(residual, 2), axis=2), 2)
    grad_increments = suffix / math.sqrt(TIME)
    return (grad_model, grad_increments)
```

```python
import math

import jax
import jax.numpy as jnp
from jax import lax
from jax.sharding import PartitionSpec as P

BF = jnp.bfloat16
F32 = jnp.float32
AXES = ("tm", "tile")


def parts(x):
    hi = x.astype(BF)
    rest = x - hi.astype(F32)
    mid = rest.astype(BF)
    low = (rest - mid.astype(F32)).astype(BF)
    return hi, mid, low


def running_sum(values, backward):
    components, line_count, step_count = values.shape
    block_size = 128
    pieces = values.reshape(components, line_count, step_count // block_size, block_size)
    rows_index = lax.broadcasted_iota(jnp.int32, (block_size, block_size), 0)
    cols_index = lax.broadcasted_iota(jnp.int32, (block_size, block_size), 1)
    if backward:
        triangle = (rows_index >= cols_index).astype(F32)
    else:
        triangle = (rows_index <= cols_index).astype(F32)
    within = jnp.matmul(pieces, triangle, precision=lax.Precision.HIGHEST)
    count = step_count // block_size
    if backward:
        block_total = within[..., 0]
        carry = [sum([block_total[..., j] for j in range(i + 1, count)], jnp.zeros_like(block_total[..., 0])) for i in range(count)]
    else:
        block_total = within[..., -1]
        carry = [sum([block_total[..., j] for j in range(i)], jnp.zeros_like(block_total[..., 0])) for i in range(count)]
    offsets = jnp.stack(carry, axis=-1)
    return (within + offsets[..., None]).reshape(values.shape)


def swap(x, axes):
    return lax.all_to_all(x, axes, split_axis=0, concat_axis=0, tiled=True)


def beyond(part, backward):
    count = lax.axis_size("tm")
    place = lax.axis_index("tm")
    everyone = swap(jnp.broadcast_to(part[None], (count,) + part.shape), "tm")
    order = jnp.arange(count)
    keep = (order > place) if backward else (order < place)
    return jnp.sum(jnp.where(keep[:, None, None], everyone, 0.0), axis=0)


def shards(observed, increments, model, kernel, tile_index, station_of, line_length):
    components, line_count, step_count = observed.shape
    tiles_here = kernel.shape[0]
    tile_width = kernel.shape[-1]
    time_devices = lax.axis_size("tm")
    device_count = time_devices * lax.axis_size("tile")
    station_count = tiles_here * device_count
    row_count = line_count * step_count
    capacity = 2 * row_count // station_count
    total_steps = step_count * time_devices
    line_total = line_count * lax.axis_size("tile")
    station_gain = 1.0 / math.sqrt(line_total * total_steps / (station_count * tile_width))
    own_index = lax.axis_index("tm")

    own_cells = jnp.broadcast_to(model.astype(BF)[None], (device_count,) + model.shape)
    whole_model = swap(own_cells, AXES).reshape(-1, tile_width)

    partial_walk = running_sum(increments, False)
    offset = partial_walk + beyond(partial_walk[:, :, -1], False)[:, :, None] - observed
    positions = own_index * step_count + jnp.arange(step_count, dtype=jnp.int32)
    inside = (positions[None, :] < line_length[:, None]).reshape(row_count)

    flat_station = station_of.reshape(row_count)
    tile_of_row = flat_station // tile_width
    label = jnp.where(inside, flat_station % tile_width + 1, 0).astype(BF)
    block = 256
    tile_hot = (tile_of_row[:, None] == jnp.arange(station_count)).astype(BF)
    blocks = tile_hot.reshape(row_count // block, block, station_count)
    order = jnp.arange(block)
    before = (order[:, None] > order[None, :]).astype(BF)
    earlier_here = jnp.einsum("ij,bjt->bit", before, blocks, preferred_element_type=F32)
    totals = jnp.sum(blocks.astype(F32), axis=1)
    block_order = jnp.arange(row_count // block)
    block_before = (block_order[:, None] > block_order[None, :]).astype(BF)
    earlier_blocks = jnp.einsum("ab,bt->at", block_before, totals.astype(BF), preferred_element_type=F32)
    rank = jnp.sum(jnp.where(blocks > 0, earlier_here + earlier_blocks[:, None, :], 0.0), axis=2)
    rank = rank.reshape(row_count).astype(jnp.int32)
    rank_hot = rank[None, :] == jnp.arange(capacity)[:, None]

    flat_offset = offset.reshape(components, row_count)
    hi, mid, low = parts(flat_offset)
    stacked = jnp.concatenate([label[None], hi, mid, low], axis=0)
    spread = jnp.where(rank_hot[None], stacked[:, None, :], jnp.zeros((), BF))
    placed = jnp.einsum("crs,st->tcr", spread, tile_hot, preferred_element_type=F32)
    n = components
    outgoing = jnp.concatenate(
        [placed[:, :1], placed[:, 1 : 1 + n] + placed[:, 1 + n : 1 + 2 * n] + placed[:, 1 + 2 * n :]], axis=1
    )
    outgoing = outgoing.reshape(device_count, tiles_here, (n + 1) * capacity)
    arrived = swap(outgoing, AXES).reshape(device_count, tiles_here, n + 1, capacity)
    arrived = jnp.transpose(arrived, (1, 2, 0, 3)).reshape(tiles_here, n + 1, device_count * capacity)
    tags, values = arrived[:, 0], arrived[:, 1:]

    chosen = whole_model[tile_index]
    predicted = jnp.einsum("skcij,skj->sci", kernel, chosen, preferred_element_type=F32)
    station_ids = jnp.arange(1, tile_width + 1, dtype=jnp.int32)
    matches = (tags.astype(jnp.int32)[:, None, :] == station_ids[:, None]).astype(BF)
    three = jnp.concatenate(parts(predicted), axis=1)
    picked = jnp.einsum("sci,sir->scr", three, matches, preferred_element_type=F32)
    picked = picked[:, :n] + picked[:, n : 2 * n] + picked[:, 2 * n :]
    answer = jnp.where(tags[:, None] > 0, picked + values, 0.0)
    three = jnp.concatenate(parts(answer), axis=1)
    sums = jnp.einsum("scr,sir->sci", three, matches, preferred_element_type=F32)
    station_sums = sums[:, :n] + sums[:, n : 2 * n] + sums[:, 2 * n :]
    station_half = (station_sums * station_gain).astype(BF)

    back = answer.astype(BF).reshape(tiles_here, n, device_count, capacity)
    back = jnp.transpose(back, (2, 0, 1, 3)).reshape(device_count, tiles_here, n * capacity)
    returned = swap(back, AXES).reshape(station_count, n, capacity)
    wide = jnp.einsum("tcr,st->crs", returned, tile_hot, preferred_element_type=F32)
    residual = jnp.sum(jnp.where(rank_hot[None], wide, 0.0), axis=1)

    contributions = jnp.einsum("skcij,sci->skj", kernel, station_half, preferred_element_type=F32)
    cell_total = model.shape[0] * device_count
    cell_hot = (jnp.arange(cell_total)[:, None] == tile_index.reshape(-1)[None, :]).astype(F32)
    local_grad = jnp.matmul(cell_hot, contributions.reshape(-1, tile_width), precision=lax.Precision.HIGHEST)
    terms = swap(local_grad.reshape((device_count,) + model.shape), AXES)
    grad_model = jnp.sum(terms, axis=0)

    residual_block = residual.reshape(components, line_count, step_count)
    partial_tail = running_sum(residual_block, True)
    remaining = beyond(partial_tail[:, :, 0], True)
    grad_increments = (partial_tail + remaining[:, :, None]) / math.sqrt(total_steps)
    return (grad_model, grad_increments)


def solution(mesh):
    in_specs = (
        P(None, "tile", "tm"),
        P(None, "tile", "tm"),
        P(("tm", "tile"), None),
        P(("tm", "tile"), None, None, None, None),
        P(("tm", "tile"), None),
        P("tile", "tm"),
        P("tile"),
    )
    out_specs = (P(("tm", "tile"), None), P(None, "tile", "tm"))
    return jax.shard_map(shards, mesh=mesh, in_specs=in_specs, out_specs=out_specs, check_vma=False)
```

```python
import functools
import math

import jax
import jax.numpy as jnp
from jax import lax
from jax.experimental import pallas as pl
from jax.experimental.pallas import tpu as pltpu
from jax.sharding import PartitionSpec as P

MESH = pl.DeviceIdType.MESH
BF = jnp.bfloat16
F32 = jnp.float32
I32 = jnp.int32
TM = 16
TILE = 8
DEV = TM * TILE
CAP = 32
SLOT = 16
COMPS = 9
LINES = 8
STEPS = 512
WIDTH = 256
HALF = 128
NNZ = 4
PAIRS = 8
LABEL = 9
LINE = 10
SPARE = 12


def iota(shape, dim):
    return lax.broadcasted_iota(I32, shape, dim)


def nn(a, b):
    return lax.dot_general(a, b, (((1,), (0,)), ((), ())), preferred_element_type=F32)


def nt(a, b):
    return lax.dot_general(a, b, (((1,), (1,)), ((), ())), preferred_element_type=F32)


def split(x, count):
    pieces = []
    for _ in range(count):
        top = x.astype(BF).astype(F32)
        pieces.append(top)
        x = x - top
    return pieces


def ones(mask):
    return jnp.where(mask, 1.0, 0.0).astype(BF)


def spare_lane(line, comp):
    return (line * 4 + comp // 4) * SLOT + SPARE + comp % 4


def body(
    obs_ref, inc_ref, model_ref, kern_ref, index_ref, station_ref, length_ref,
    grad_ref, walk_ref,
    kern_v, hot_v, spread_v, rank_v, off_v, stage_v, table_v, early_v, cell_v, adj_v, wide_v, res_v, fold_v,
    mod_out, mod_in, out1, in1, out2, in2, out3, in3,
    kern_sem, local_sem, send_sem, recv_sem,
):
    tm, tile = lax.axis_index("tm"), lax.axis_index("tile")
    me = tm * TILE + tile
    tiles = [lax.rem(tile + k, TILE) for k in range(TILE)]

    barrier = pltpu.get_barrier_semaphore()

    def greet(row, columns):
        for t in columns:
            pl.semaphore_signal(barrier, inc=1, device_id=(row, t), device_id_type=MESH)

    greet(tm, tiles[1:])

    def greet_row(i, _):
        greet(lax.rem(tm + i, TM), tiles)
        return 0

    lax.fori_loop(1, TM, greet_row, 0)
    fetch = pltpu.make_async_copy(kern_ref, kern_v, kern_sem)
    fetch.start()

    def send_row(src_of, dst, slot, row, columns):
        for t in columns:
            pltpu.make_async_remote_copy(
                src_ref=src_of(row * TILE + t), dst_ref=dst.at[me],
                send_sem=send_sem.at[slot], recv_sem=recv_sem.at[slot],
                device_id=(row, t), device_id_type=MESH,
            ).start()

    def send_all(src_of, dst, slot):
        own = pltpu.make_async_copy(src_of(me), dst.at[me], local_sem.at[slot])
        own.start()
        send_row(src_of, dst, slot, tm, tiles[1:])

        def one(i, _):
            send_row(src_of, dst, slot, lax.rem(tm + i, TM), tiles)
            return 0

        lax.fori_loop(1, TM, one, 0)
        return own

    def all_arrived(dst, slot, own):
        own.wait()
        span = dst.at[pl.ds(0, DEV - 1)]
        pltpu.make_async_copy(span, span, recv_sem.at[slot]).wait()

    def all_sent(dst, slot):
        span = dst.at[pl.ds(0, DEV - 1)]
        pltpu.make_async_copy(span, span, send_sem.at[slot]).wait()

    cells = model_ref[...]
    mod_out[...] = jnp.concatenate([cells[:, :HALF], cells[:, HALF:]], axis=0).astype(BF)

    upto = ones(iota((WIDTH, WIDTH), 0) <= iota((WIDTH, WIDTH), 1))
    steps = inc_ref[...]
    rows = COMPS * LINES
    first = jnp.concatenate(split(steps[:, :WIDTH], 3), axis=0).astype(BF)
    second = jnp.concatenate(split(steps[:, WIDTH:], 3), axis=0).astype(BF)
    first, second = nn(first, upto), nn(second, upto)
    first = first[:rows] + first[rows : 2 * rows] + first[2 * rows :]
    second = second[:rows] + second[rows : 2 * rows] + second[2 * rows :]
    second = second + first[:, WIDTH - 1 :]
    totals = second[:, WIDTH - 1 :]
    first = first - obs_ref[:, :WIDTH]
    second = second - obs_ref[:, WIDTH:]
    for j, part in enumerate((first[:, :HALF], first[:, HALF:], second[:, :HALF], second[:, HALF:])):
        off_v[pl.ds(j * DEV, rows), :] = part
        off_v[pl.ds(j * DEV + rows, DEV - rows), :] = jnp.zeros((DEV - rows, HALF), F32)

    pl.semaphore_wait(barrier, DEV - 1)
    own_mod = send_all(lambda p: mod_out, mod_in, 0)

    def one_line(l, base):
        lanes = pl.ds(pl.multiple_of(l * STEPS, STEPS), STEPS)
        station = station_ref[pl.ds(l, 1), :]
        owner = station // WIDTH
        inner = station % WIDTH
        line_place = (owner % 2) * HALF + owner // 2
        hit = iota((WIDTH, STEPS), 0) == line_place
        hot = ones(hit)
        hot_v[:, lanes] = hot
        ranks = []
        for h in range(2):
            part = slice(h * WIDTH, (h + 1) * WIDTH)
            count = nn(hot[:, part], upto)
            ranks.append(jnp.sum(jnp.where(hit[:, part], count + base, 0.0), axis=0, keepdims=True))
            base = base + count[:, WIDTH - 1 :]
        rank = jnp.concatenate(ranks, axis=1) - 1.0
        rank_v[pl.ds(l, 1), :] = rank
        position = tm * STEPS + iota((1, STEPS), 1)
        label = jnp.where(position < length_ref[l], inner + 1, 0).astype(F32)
        comp = iota((SLOT, STEPS), 0)
        values = jnp.concatenate([off_v[pl.ds(j * DEV + l, SLOT, stride=LINES), :] for j in range(4)], axis=1)
        values = jnp.where(comp == LABEL, label, values)
        values = jnp.where(comp == LINE, l.astype(F32), values)
        for r in range(CAP):
            spread_v[pl.ds(r * SLOT, SLOT), lanes] = jnp.where(rank == float(r), values, 0.0).astype(BF)
        return base

    lax.fori_loop(0, LINES, one_line, jnp.zeros((WIDTH, 1), F32))

    placed = nt(hot_v[...], spread_v[...])
    row = iota((rows, CAP * SLOT), 0)
    at_spare = iota((rows, CAP * SLOT), 1) == spare_lane(row % LINES, row // LINES)
    for s, part in enumerate(split(totals, 2)):
        extra = jnp.sum(jnp.where(at_spare, part, 0.0), axis=0, keepdims=True)
        half = placed[s * HALF : (s + 1) * HALF] + extra
        for g in range(4):
            stage_v[pl.ds(s * 4 + g, DEV, stride=8), :] = half[:, g * HALF : (g + 1) * HALF]

    def pack(dst):
        dst[...] = stage_v[...].reshape(DEV, 8, HALF).astype(BF)

    def unpack(src):
        stage_v[...] = src[...].astype(F32).reshape(DEV * 8, HALF)

    pack(out1)
    own1 = send_all(lambda p: out1.at[p], in1, 1)

    fetch.wait()
    all_arrived(mod_in, 0, own_mod)
    pair_row = iota((SLOT, DEV * 8), 0)
    pair_lane = iota((SLOT, DEV * 8), 1)
    base_row = jnp.full((SLOT, DEV * 8), -8, I32)
    for q in range(PAIRS):
        cell = index_ref[q // NNZ, q % NNZ]
        base_row = jnp.where(pair_row == q, (cell // 4) * 8 + cell % 4, base_row)
    every = mod_in[...].reshape(DEV * 8, HALF)
    chosen = jnp.concatenate([nn(ones(pair_lane == base_row + 4 * h), every) for h in range(2)], axis=1)
    cell_v[...] = chosen
    comp_row = iota((SLOT, WIDTH), 0)
    predicted = []
    for s in range(2):

        def forward(k, total):
            vector = cell_v[pl.ds(s * NNZ + k, 1), :]
            for c in range(COMPS):
                left = jnp.where(comp_row == c, vector, 0.0).astype(BF)
                total = total + nt(left, kern_v[(s * NNZ + k) * COMPS + c])
            return total

        predicted.append(lax.fori_loop(0, NNZ, forward, jnp.zeros((SLOT, WIDTH), F32)))

    all_arrived(in1, 1, own1)
    unpack(in1)
    for s in range(2):
        for g in range(4):
            table_v[s, pl.ds(g * HALF, HALF), :] = stage_v[pl.ds(s * 4 + g, DEV, stride=8), :].T
    q_row = iota((DEV, CAP * SLOT), 0)
    pick = ones(
        (iota((DEV, CAP * SLOT), 1) == spare_lane(q_row // SLOT, q_row % SLOT)) & (q_row % SLOT < COMPS)
    )
    q_lane = iota((CAP * SLOT, DEV), 1)
    put = ones(
        (iota((CAP * SLOT, DEV), 0) == spare_lane(q_lane // SLOT, q_lane % SLOT)) & (q_lane % SLOT < COMPS)
    )
    source, target = iota((DEV, DEV), 0), iota((DEV, DEV), 1)
    same_lines = source % TILE == target % TILE
    before = ones(same_lines & (source // TILE < target // TILE))
    after = ones(same_lines & (source // TILE > target // TILE))
    early = jnp.zeros((DEV, DEV), F32)
    for s in range(2):
        part = nn(pick, table_v[s].astype(BF))
        early = early + nn(part.astype(BF), before)
    early_v[...] = early

    lane_count = 2 * HALF
    slot_row = iota((SLOT, lane_count), 0)
    station_row = iota((WIDTH, lane_count), 0)
    sums = []
    line_sums = [jnp.zeros((SLOT, HALF), F32) for _ in range(LINES)]
    for s in range(2):
        three = jnp.concatenate(split(predicted[s], 3), axis=0).astype(BF)

        def slots(i, carry):
            total = carry[0]
            lines = list(carry[1:])
            start = pl.multiple_of(i * 2 * SLOT, 2 * SLOT)
            got = jnp.concatenate(
                [table_v[s, pl.ds(start, SLOT), :], table_v[s, pl.ds(start + SLOT, SLOT), :]], axis=1
            )
            label = got[LABEL : LABEL + 1]
            line = got[LINE : LINE + 1]
            match = ones(station_row == label.astype(I32) - 1)
            picked = nn(three, match)
            picked = picked[:SLOT] + picked[SLOT : 2 * SLOT] + picked[2 * SLOT :]
            value = picked + got
            for l in range(LINES):
                walk = early_v[pl.ds(l * SLOT, SLOT), :]
                value = value + jnp.where(line == float(l), jnp.concatenate([walk, walk], axis=1), 0.0)
            value = jnp.where((label > 0.0) & (slot_row < COMPS), value, 0.0)
            res_v[s, pl.ds(start, SLOT), :] = value[:, :HALF]
            res_v[s, pl.ds(start + SLOT, SLOT), :] = value[:, HALF:]
            for l in range(LINES):
                mine = jnp.where(line == float(l), value, 0.0)
                lines[l] = lines[l] + mine[:, :HALF] + mine[:, HALF:]
            total = total + nt(jnp.concatenate(split(value, 3), axis=0).astype(BF), match)
            return (total, *lines)

        carry = lax.fori_loop(
            0, CAP // 2, slots, (jnp.zeros((3 * SLOT, WIDTH), F32), *line_sums)
        )
        sums.append(carry[0][:SLOT] + carry[0][SLOT : 2 * SLOT] + carry[0][2 * SLOT :])
        line_sums = list(carry[1:])

    gathered = jnp.concatenate(line_sums, axis=0)
    three = nn(jnp.concatenate(split(gathered, 3), axis=0).astype(BF), after)
    beyond = three[:DEV] + three[DEV : 2 * DEV] + three[2 * DEV :]
    for s, part in enumerate(split(beyond, 2)):
        full = res_v[s] + nn(put, part.astype(BF))
        for g in range(4):
            stage_v[pl.ds(s * 4 + g, DEV, stride=8), :] = full[g * HALF : (g + 1) * HALF, :].T
    pack(out2)
    own2 = send_all(lambda p: out2.at[p], in2, 2)

    gain = 1.0 / math.sqrt(LINES * TILE * STEPS * TM / (2 * DEV * WIDTH))
    for s in range(2):
        adj_v[s] = (sums[s] * gain).astype(BF).astype(F32)
    contributions = jnp.zeros((SLOT, WIDTH), F32)
    for s in range(2):

        def adjoint(k, total):
            for c in range(COMPS):
                left = jnp.where(comp_row == s * NNZ + k, adj_v[s, pl.ds(c, 1), :], 0.0).astype(BF)
                total = total + nn(left, kern_v[(s * NNZ + k) * COMPS + c])
            return total

        contributions = lax.fori_loop(0, NNZ, adjoint, contributions)
    pieces = [piece[:PAIRS] for piece in split(contributions, 2)]
    stack = [piece[:, h * HALF : (h + 1) * HALF] for h in range(2) for piece in pieces]
    stack = jnp.concatenate(stack + [jnp.zeros((HALF - 4 * PAIRS, HALF), F32)], axis=0).astype(BF)
    lane = iota((1, HALF), 1)
    goal = jnp.full((1, HALF), -8, I32)
    for q in range(PAIRS):
        cell = index_ref[q // NNZ, q % NNZ]
        goal = jnp.where(lane % PAIRS == q, (cell // 4) * 8 + cell % 4, goal)
    goal = jnp.where(lane < 4 * PAIRS, goal + 4 * (lane // (2 * PAIRS)), -8)
    stage_v[...] = nn(ones(iota((DEV * 8, HALF), 0) == goal), stack)
    pack(out3)
    own3 = send_all(lambda p: out3.at[p], in3, 3)

    all_arrived(in2, 2, own2)
    unpack(in2)
    for s in range(2):
        for g in range(4):
            wide_v[pl.ds(g * HALF, HALF), pl.ds(s * HALF, HALF)] = (
                stage_v[pl.ds(s * 4 + g, DEV, stride=8), :].T.astype(BF)
            )
    rest = jnp.sum(nn(pick, wide_v[...]), axis=1, keepdims=True)

    def collect(l, _):
        lanes = pl.ds(pl.multiple_of(l * STEPS, STEPS), STEPS)
        every = nn(wide_v[...], hot_v[:, lanes])
        rank = rank_v[pl.ds(l, 1), :]
        value = jnp.zeros((SLOT, STEPS), F32)
        for r in range(CAP):
            value = value + jnp.where(rank == float(r), every[r * SLOT : (r + 1) * SLOT], 0.0)
        fold_v[pl.ds(pl.multiple_of(l * SLOT, SLOT), SLOT), :] = value
        return 0

    lax.fori_loop(0, LINES, collect, 0)
    onward = ones(iota((WIDTH, WIDTH), 0) >= iota((WIDTH, WIDTH), 1))
    late = nn(fold_v[:, WIDTH:].astype(BF), onward) + rest
    soon = nn(fold_v[:, :WIDTH].astype(BF), onward) + late[:, :1]
    scale = 1.0 / math.sqrt(STEPS * TM)
    for j, part in enumerate((soon[:, :HALF], soon[:, HALF:], late[:, :HALF], late[:, HALF:])):
        for l in range(LINES):
            off_v[pl.ds(j * DEV + l, SLOT, stride=LINES), :] = part[l * SLOT : (l + 1) * SLOT] * scale
        walk_ref[:, pl.ds(j * HALF, HALF)] = off_v[pl.ds(j * DEV, rows), :]

    all_arrived(in3, 3, own3)
    grad = jnp.sum(in3[...].astype(F32), axis=0)
    grad_ref[...] = jnp.concatenate([grad[:4], grad[4:]], axis=1)
    for slot, dst in enumerate((mod_in, in1, in2, in3)):
        all_sent(dst, slot)


def shards(observed, increments, model, kernel, tile_index, station_of, line_length):
    rows = COMPS * LINES
    vmem = pl.BlockSpec(memory_space=pltpu.VMEM)
    smem = pl.BlockSpec(memory_space=pltpu.SMEM)
    message = pltpu.VMEM((DEV, 8, HALF), BF)
    grad_model, walk = pl.pallas_call(
        body,
        out_shape=(
            jax.ShapeDtypeStruct((4, WIDTH), F32),
            jax.ShapeDtypeStruct((rows, STEPS), F32),
        ),
        in_specs=[vmem, vmem, vmem, pl.BlockSpec(memory_space=pl.ANY), smem, vmem, smem],
        out_specs=(vmem, vmem),
        scratch_shapes=[
            pltpu.VMEM((PAIRS * COMPS, WIDTH, WIDTH), BF),
            pltpu.VMEM((WIDTH, LINES * STEPS), BF),
            pltpu.VMEM((CAP * SLOT, LINES * STEPS), BF),
            pltpu.VMEM((LINES, STEPS), F32),
            pltpu.VMEM((4 * DEV, HALF), F32),
            pltpu.VMEM((DEV * 8, HALF), F32),
            pltpu.VMEM((2, CAP * SLOT, HALF), F32),
            pltpu.VMEM((DEV, DEV), F32),
            pltpu.VMEM((SLOT, WIDTH), F32),
            pltpu.VMEM((2, SLOT, WIDTH), F32),
            pltpu.VMEM((CAP * SLOT, WIDTH), BF),
            pltpu.VMEM((2, CAP * SLOT, HALF), F32),
            pltpu.VMEM((DEV, STEPS), F32),
            pltpu.VMEM((8, HALF), BF),
            message, message, message, message, message, message, message,
            pltpu.SemaphoreType.DMA,
            pltpu.SemaphoreType.DMA((4,)),
            pltpu.SemaphoreType.DMA((4,)),
            pltpu.SemaphoreType.DMA((4,)),
        ],
        compiler_params=pltpu.CompilerParams(
            collective_id=0, has_side_effects=True, vmem_limit_bytes=48 * 1024 * 1024
        ),
        name="invert",
    )(
        observed.reshape(rows, STEPS),
        increments.reshape(rows, STEPS),
        model,
        kernel.reshape(PAIRS * COMPS, WIDTH, WIDTH),
        tile_index,
        station_of,
        line_length,
    )
    return grad_model, walk.reshape(COMPS, LINES, STEPS)


def solution(mesh):
    in_specs = (
        P(None, "tile", "tm"),
        P(None, "tile", "tm"),
        P(("tm", "tile"), None),
        P(("tm", "tile"), None, None, None, None),
        P(("tm", "tile"), None),
        P("tile", "tm"),
        P("tile"),
    )
    out_specs = (P(("tm", "tile"), None), P(None, "tile", "tm"))
    return jax.shard_map(shards, mesh=mesh, in_specs=in_specs, out_specs=out_specs, check_vma=False)
```

```python
import functools
import math

import jax
import jax.numpy as jnp
from jax import lax
from jax.experimental import pallas as pl
from jax.experimental.pallas import tpu as pltpu
from jax.sharding import PartitionSpec as P

MESH = pl.DeviceIdType.MESH
BF = jnp.bfloat16
F32 = jnp.float32
I32 = jnp.int32
TM = 16
TILE = 8
DEV = TM * TILE
CAP = 32
SLOT = 16
COMPS = 9
CHUNK = 64
LINES = 8
STEPS = 512
WIDTH = 256
HALF = 128
NNZ = 4
PAIRS = 8
LABEL = 9
LINE = 10
SPARE = 12
GRID = sorted(((x, y) for x in range(4) for y in range(4)), key=lambda o: -sum(min(v, 4 - v) for v in o))
COLUMNS = (4, 5, 3, 2, 6, 7, 1, 0)


def iota(shape, dim):
    return lax.broadcasted_iota(I32, shape, dim)


def nn(a, b):
    return lax.dot_general(a, b, (((1,), (0,)), ((), ())), preferred_element_type=F32)


def nt(a, b):
    return lax.dot_general(a, b, (((1,), (1,)), ((), ())), preferred_element_type=F32)


def split(x, count):
    pieces = []
    for _ in range(count):
        top = x.astype(BF).astype(F32)
        pieces.append(top)
        x = x - top
    return pieces


def ones(mask):
    return jnp.where(mask, 1.0, 0.0).astype(BF)


def spare_lane(line, comp):
    return (line * 4 + comp // 4) * SLOT + SPARE + comp % 4


def body(
    obs_hbm, inc_hbm, model_hbm, kern_ref, index_hbm, station_hbm, length_hbm,
    grad_ref, walk_ref,
    obs_ref, inc_ref, model_ref, index_ref, station_ref, length_ref,
    kern_v, hot_v, spread_v, rank_v, off_v, stage_v, table_v, early_v, cell_v, pred_v, adj_v, wide_v, res_v, fold_v,
    mod_out, mod_in, out1, in1, out2, in2, out3, in3,
    load_sem, kern_sem, local_sem, send_sem, recv_sem,
):
    tm, tile = lax.axis_index("tm"), lax.axis_index("tile")
    me = tm * TILE + tile
    tiles = [lax.rem(tile + k, TILE) for k in COLUMNS]

    loads = [
        pltpu.make_async_copy(hbm, ref, load_sem.at[i])
        for i, (hbm, ref) in enumerate(
            (
                (inc_hbm, inc_ref), (obs_hbm, obs_ref), (model_hbm, model_ref),
                (station_hbm, station_ref), (length_hbm, length_ref), (index_hbm, index_ref),
            )
        )
    ]
    for load in loads:
        load.start()
    barrier = pltpu.get_barrier_semaphore()

    def greet(row, columns):
        for t in columns:
            pl.semaphore_signal(barrier, inc=1, device_id=(row, t), device_id_type=MESH)

    greet(tm, tiles[:-1])

    def greet_row(i, _):
        greet(lax.rem(tm + i, TM), tiles)
        return 0

    lax.fori_loop(1, TM, greet_row, 0)
    fetch = pltpu.make_async_copy(kern_ref, kern_v, kern_sem)
    fetch.start()

    def send_all(src_of, dst, slot):
        own = pltpu.make_async_copy(src_of(me), dst.at[me], local_sem.at[slot])
        own.start()
        for dx, dy in GRID:
            row = lax.rem(tm // 4 + dx, 4) * 4 + lax.rem(lax.rem(tm, 4) + dy, 4)
            for k, t in zip(COLUMNS, tiles):
                if (dx, dy, k) != (0, 0, 0):
                    pltpu.make_async_remote_copy(
                        src_ref=src_of(row * TILE + t), dst_ref=dst.at[me],
                        send_sem=send_sem.at[slot], recv_sem=recv_sem.at[slot],
                        device_id=(row, t), device_id_type=MESH,
                    ).start()
        return own

    def all_arrived(dst, slot, own):
        own.wait()
        span = dst.at[pl.ds(0, DEV - 1)]
        pltpu.make_async_copy(span, span, recv_sem.at[slot]).wait()

    def all_sent(dst, slot):
        span = dst.at[pl.ds(0, DEV - 1)]
        pltpu.make_async_copy(span, span, send_sem.at[slot]).wait()

    for load in loads:
        load.wait()
    cells = model_ref[...]
    mod_out[...] = jnp.concatenate([cells[:, :HALF], cells[:, HALF:]], axis=0).astype(BF)

    upto = ones(iota((WIDTH, WIDTH), 0) <= iota((WIDTH, WIDTH), 1))
    steps = inc_ref[...]
    rows = COMPS * LINES
    first = jnp.concatenate(split(steps[:, :WIDTH], 3), axis=0).astype(BF)
    second = jnp.concatenate(split(steps[:, WIDTH:], 3), axis=0).astype(BF)
    first, second = nn(first, upto), nn(second, upto)
    first = first[:rows] + first[rows : 2 * rows] + first[2 * rows :]
    second = second[:rows] + second[rows : 2 * rows] + second[2 * rows :]
    second = second + first[:, WIDTH - 1 :]
    totals = second[:, WIDTH - 1 :]
    first = first - obs_ref[:, :WIDTH]
    second = second - obs_ref[:, WIDTH:]
    for j, part in enumerate((first[:, :HALF], first[:, HALF:], second[:, :HALF], second[:, HALF:])):
        off_v[pl.ds(j * DEV, rows), :] = part
        off_v[pl.ds(j * DEV + rows, DEV - rows), :] = jnp.zeros((DEV - rows, HALF), F32)

    def one_line(l, base):
        lanes = pl.ds(pl.multiple_of(l * STEPS, STEPS), STEPS)
        station = station_ref[pl.ds(l, 1), :]
        owner = station // WIDTH
        inner = station % WIDTH
        line_place = (owner % 2) * HALF + owner // 2
        hit = iota((WIDTH, STEPS), 0) == line_place
        hot = ones(hit)
        hot_v[:, lanes] = hot
        ranks = []
        for h in range(2):
            part = slice(h * WIDTH, (h + 1) * WIDTH)
            count = nn(hot[:, part], upto)
            ranks.append(jnp.sum(jnp.where(hit[:, part], count + base, 0.0), axis=0, keepdims=True))
            base = base + count[:, WIDTH - 1 :]
        rank = jnp.concatenate(ranks, axis=1) - 1.0
        rank_v[pl.ds(l, 1), :] = rank
        position = tm * STEPS + iota((1, STEPS), 1)
        label = jnp.where(position < length_ref[l], inner + 1, 0).astype(F32)
        comp = iota((SLOT, STEPS), 0)
        values = jnp.concatenate([off_v[pl.ds(j * DEV + l, SLOT, stride=LINES), :] for j in range(4)], axis=1)
        values = jnp.where(comp == LABEL, label, values)
        values = jnp.where(comp == LINE, l.astype(F32), values)
        for r in range(CAP):
            spread_v[pl.ds(r * SLOT, SLOT), lanes] = jnp.where(rank == float(r), values, 0.0).astype(BF)
        return base

    lax.fori_loop(0, LINES, one_line, jnp.zeros((WIDTH, 1), F32))

    placed = nt(hot_v[...], spread_v[...])
    row = iota((rows, CAP * SLOT), 0)
    at_spare = iota((rows, CAP * SLOT), 1) == spare_lane(row % LINES, row // LINES)
    for s, part in enumerate(split(totals, 2)):
        extra = jnp.sum(jnp.where(at_spare, part, 0.0), axis=0, keepdims=True)
        half = placed[s * HALF : (s + 1) * HALF] + extra
        for g in range(4):
            stage_v[pl.ds(s * 4 + g, DEV, stride=8), :] = half[:, g * HALF : (g + 1) * HALF]

    def pack(dst):
        dst[...] = stage_v[...].reshape(DEV, 8, HALF).astype(BF)

    def unpack(src):
        stage_v[...] = src[...].astype(F32).reshape(DEV * 8, HALF)

    pack(out1)
    pl.semaphore_wait(barrier, DEV - 1)
    own_mod = send_all(lambda p: mod_out, mod_in, 0)
    own1 = send_all(lambda p: out1.at[p], in1, 1)

    fetch.wait()
    all_arrived(mod_in, 0, own_mod)
    pair_row = iota((SLOT, DEV * 8), 0)
    pair_lane = iota((SLOT, DEV * 8), 1)
    base_row = jnp.full((SLOT, DEV * 8), -8, I32)
    for q in range(PAIRS):
        cell = index_ref[q // NNZ, q % NNZ]
        base_row = jnp.where(pair_row == q, (cell // 4) * 8 + cell % 4, base_row)
    every = mod_in[...].reshape(DEV * 8, HALF)
    chosen = jnp.concatenate([nn(ones(pair_lane == base_row + 4 * h), every) for h in range(2)], axis=1)
    cell_v[...] = chosen
    comp_row = iota((SLOT, HALF), 0)
    for s in range(2):
        vectors = [cell_v[pl.ds(s * NNZ + k, 1), :] for k in range(NNZ)]

        def forward(c, halves):
            sums = []
            for i in range(0, WIDTH, CHUNK):
                total = jnp.zeros((CHUNK, HALF), F32)
                for k in range(NNZ):
                    block = kern_v[(s * NNZ + k) * COMPS + c, pl.ds(i, CHUNK), :].astype(F32) * vectors[k]
                    total = total + block[:, :HALF] + block[:, HALF:]
                sums.append(total)
            rows_here = []
            for h in range(2):
                tall = jnp.concatenate(sums[h * HALF // CHUNK : (h + 1) * HALF // CHUNK], axis=0).T
                rows_here.append(jnp.where(comp_row == c, jnp.sum(tall, axis=0, keepdims=True), halves[h]))
            return tuple(rows_here)

        halves = lax.fori_loop(0, COMPS, forward, (jnp.zeros((SLOT, HALF), F32),) * 2)
        for h in range(2):
            pred_v[s, :, pl.ds(h * HALF, HALF)] = halves[h]

    all_arrived(in1, 1, own1)
    unpack(in1)
    for s in range(2):
        for g in range(4):
            table_v[s, pl.ds(g * HALF, HALF), :] = stage_v[pl.ds(s * 4 + g, DEV, stride=8), :].T
    q_row = iota((DEV, CAP * SLOT), 0)
    pick = ones(
        (iota((DEV, CAP * SLOT), 1) == spare_lane(q_row // SLOT, q_row % SLOT)) & (q_row % SLOT < COMPS)
    )
    q_lane = iota((CAP * SLOT, DEV), 1)
    put = ones(
        (iota((CAP * SLOT, DEV), 0) == spare_lane(q_lane // SLOT, q_lane % SLOT)) & (q_lane % SLOT < COMPS)
    )
    source, target = iota((DEV, DEV), 0), iota((DEV, DEV), 1)
    same_lines = source % TILE == target % TILE
    before = ones(same_lines & (source // TILE < target // TILE))
    after = ones(same_lines & (source // TILE > target // TILE))
    early = jnp.zeros((DEV, DEV), F32)
    for s in range(2):
        part = nn(pick, table_v[s].astype(BF))
        early = early + nn(part.astype(BF), before)
    early_v[...] = early

    lane_count = 2 * HALF
    slot_row = iota((SLOT, lane_count), 0)
    station_row = iota((WIDTH, lane_count), 0)
    tables = [[pred_v[s, :, pl.ds(h * HALF, HALF)] for h in range(2)] for s in range(2)]

    def slots(i, carry):
        totals = list(carry[:2])
        lines = list(carry[2:])
        start = pl.multiple_of(i * 2 * SLOT, 2 * SLOT)
        for s in range(2):
            pair = [table_v[s, pl.ds(start + j * SLOT, SLOT), :] for j in range(2)]
            got = jnp.concatenate(pair, axis=1)
            label = got[LABEL : LABEL + 1]
            line = got[LINE : LINE + 1]
            match = ones(station_row == label.astype(I32) - 1)
            picked = []
            for part in pair:
                at = jnp.broadcast_to(jnp.maximum(part[LABEL : LABEL + 1].astype(I32) - 1, 0), (SLOT, HALF))
                lane = at % HALF
                low = jnp.take_along_axis(tables[s][0], lane, axis=1)
                high = jnp.take_along_axis(tables[s][1], lane, axis=1)
                picked.append(jnp.where(at >= HALF, high, low))
            value = jnp.concatenate(picked, axis=1) + got
            for l in range(LINES):
                walk = early_v[pl.ds(l * SLOT, SLOT), :]
                value = value + jnp.where(line == float(l), jnp.concatenate([walk, walk], axis=1), 0.0)
            value = jnp.where((label > 0.0) & (slot_row < COMPS), value, 0.0)
            res_v[s, pl.ds(start, SLOT), :] = value[:, :HALF]
            res_v[s, pl.ds(start + SLOT, SLOT), :] = value[:, HALF:]
            for l in range(LINES):
                mine = jnp.where(line == float(l), value, 0.0)
                lines[l] = lines[l] + mine[:, :HALF] + mine[:, HALF:]
            totals[s] = totals[s] + nt(jnp.concatenate(split(value, 3), axis=0).astype(BF), match)
        return (*totals, *lines)

    carry = lax.fori_loop(
        0, CAP // 2, slots,
        (*[jnp.zeros((3 * SLOT, WIDTH), F32)] * 2, *[jnp.zeros((SLOT, HALF), F32)] * LINES),
    )
    sums = [total[:SLOT] + total[SLOT : 2 * SLOT] + total[2 * SLOT :] for total in carry[:2]]
    line_sums = list(carry[2:])

    gathered = jnp.concatenate(line_sums, axis=0)
    three = nn(jnp.concatenate(split(gathered, 3), axis=0).astype(BF), after)
    beyond = three[:DEV] + three[DEV : 2 * DEV] + three[2 * DEV :]
    for s, part in enumerate(split(beyond, 2)):
        full = res_v[s] + nn(put, part.astype(BF))
        for g in range(4):
            stage_v[pl.ds(s * 4 + g, DEV, stride=8), :] = full[g * HALF : (g + 1) * HALF, :].T
    pack(out2)
    own2 = send_all(lambda p: out2.at[p], in2, 2)

    gain = 1.0 / math.sqrt(LINES * TILE * STEPS * TM / (2 * DEV * WIDTH))
    filler = jnp.zeros((HALF - SLOT, WIDTH), F32)
    for s in range(2):
        sheet = jnp.concatenate([(sums[s] * gain).astype(BF).astype(F32), filler], axis=0)
        adj_v[s] = jnp.concatenate([sheet[:, :HALF].T, sheet[:, HALF:].T], axis=0)
    contributions = []
    for s in range(2):

        def adjoint(i, totals):
            totals = list(totals)
            start = pl.multiple_of(i * CHUNK, CHUNK)
            weights = adj_v[s, pl.ds(start, CHUNK), :]
            for c in range(COMPS):
                weight = jnp.broadcast_to(weights[:, c : c + 1], (CHUNK, WIDTH))
                for k in range(NNZ):
                    block = kern_v[(s * NNZ + k) * COMPS + c, pl.ds(start, CHUNK), :].astype(F32) * weight
                    totals[k] = totals[k] + jnp.sum(block.reshape(CHUNK // 8, 8, WIDTH), axis=0)
            return tuple(totals)

        totals = lax.fori_loop(0, WIDTH // CHUNK, adjoint, (jnp.zeros((8, WIDTH), F32),) * NNZ)
        contributions += [jnp.sum(total, axis=0, keepdims=True) for total in totals]
    contributions = jnp.concatenate(contributions, axis=0)
    pieces = split(contributions, 2)
    stack = [piece[:, h * HALF : (h + 1) * HALF] for h in range(2) for piece in pieces]
    stack = jnp.concatenate(stack + [jnp.zeros((HALF - 4 * PAIRS, HALF), F32)], axis=0).astype(BF)
    lane = iota((1, HALF), 1)
    goal = jnp.full((1, HALF), -8, I32)
    for q in range(PAIRS):
        cell = index_ref[q // NNZ, q % NNZ]
        goal = jnp.where(lane % PAIRS == q, (cell // 4) * 8 + cell % 4, goal)
    goal = jnp.where(lane < 4 * PAIRS, goal + 4 * (lane // (2 * PAIRS)), -8)
    stage_v[...] = nn(ones(iota((DEV * 8, HALF), 0) == goal), stack)
    pack(out3)
    own3 = send_all(lambda p: out3.at[p], in3, 3)

    all_arrived(in2, 2, own2)
    unpack(in2)
    for s in range(2):
        for g in range(4):
            wide_v[pl.ds(g * HALF, HALF), pl.ds(s * HALF, HALF)] = (
                stage_v[pl.ds(s * 4 + g, DEV, stride=8), :].T.astype(BF)
            )
    rest = jnp.sum(nn(pick, wide_v[...]), axis=1, keepdims=True)

    def collect(l, _):
        lanes = pl.ds(pl.multiple_of(l * STEPS, STEPS), STEPS)
        every = nn(wide_v[...], hot_v[:, lanes])
        rank = rank_v[pl.ds(l, 1), :]
        value = jnp.zeros((SLOT, STEPS), F32)
        for r in range(CAP):
            value = value + jnp.where(rank == float(r), every[r * SLOT : (r + 1) * SLOT], 0.0)
        fold_v[pl.ds(pl.multiple_of(l * SLOT, SLOT), SLOT), :] = value
        return 0

    lax.fori_loop(0, LINES, collect, 0)
    onward = ones(iota((WIDTH, WIDTH), 0) >= iota((WIDTH, WIDTH), 1))
    late = nn(fold_v[:, WIDTH:].astype(BF), onward) + rest
    soon = nn(fold_v[:, :WIDTH].astype(BF), onward) + late[:, :1]
    scale = 1.0 / math.sqrt(STEPS * TM)
    for j, part in enumerate((soon[:, :HALF], soon[:, HALF:], late[:, :HALF], late[:, HALF:])):
        for l in range(LINES):
            off_v[pl.ds(j * DEV + l, SLOT, stride=LINES), :] = part[l * SLOT : (l + 1) * SLOT] * scale
        walk_ref[:, pl.ds(j * HALF, HALF)] = off_v[pl.ds(j * DEV, rows), :]

    all_arrived(in3, 3, own3)
    grad = jnp.sum(in3[...].astype(F32), axis=0)
    grad_ref[...] = jnp.concatenate([grad[:4], grad[4:]], axis=1)
    for slot, dst in enumerate((mod_in, in1, in2, in3)):
        all_sent(dst, slot)


def shards(observed, increments, model, kernel, tile_index, station_of, line_length):
    rows = COMPS * LINES
    vmem = pl.BlockSpec(memory_space=pltpu.VMEM)
    message = pltpu.VMEM((DEV, 8, HALF), BF)
    grad_model, walk = pl.pallas_call(
        body,
        out_shape=(
            jax.ShapeDtypeStruct((4, WIDTH), F32),
            jax.ShapeDtypeStruct((rows, STEPS), F32),
        ),
        in_specs=[pl.BlockSpec(memory_space=pl.ANY)] * 7,
        out_specs=(vmem, vmem),
        scratch_shapes=[
            pltpu.VMEM((rows, STEPS), F32),
            pltpu.VMEM((rows, STEPS), F32),
            pltpu.VMEM((4, WIDTH), F32),
            pltpu.SMEM((2, NNZ), I32),
            pltpu.VMEM((LINES, STEPS), I32),
            pltpu.SMEM((LINES,), I32),
            pltpu.VMEM((PAIRS * COMPS, WIDTH, WIDTH), BF),
            pltpu.VMEM((WIDTH, LINES * STEPS), BF),
            pltpu.VMEM((CAP * SLOT, LINES * STEPS), BF),
            pltpu.VMEM((LINES, STEPS), F32),
            pltpu.VMEM((4 * DEV, HALF), F32),
            pltpu.VMEM((DEV * 8, HALF), F32),
            pltpu.VMEM((2, CAP * SLOT, HALF), F32),
            pltpu.VMEM((DEV, DEV), F32),
            pltpu.VMEM((SLOT, WIDTH), F32),
            pltpu.VMEM((2, SLOT, WIDTH), F32),
            pltpu.VMEM((2, WIDTH, HALF), F32),
            pltpu.VMEM((CAP * SLOT, WIDTH), BF),
            pltpu.VMEM((2, CAP * SLOT, HALF), F32),
            pltpu.VMEM((DEV, STEPS), F32),
            pltpu.VMEM((8, HALF), BF),
            message, message, message, message, message, message, message,
            pltpu.SemaphoreType.DMA((6,)),
            pltpu.SemaphoreType.DMA,
            pltpu.SemaphoreType.DMA((4,)),
            pltpu.SemaphoreType.DMA((4,)),
            pltpu.SemaphoreType.DMA((4,)),
        ],
        compiler_params=pltpu.CompilerParams(
            collective_id=0, has_side_effects=True, vmem_limit_bytes=60 * 1024 * 1024
        ),
        name="invert",
    )(
        observed.reshape(rows, STEPS),
        increments.reshape(rows, STEPS),
        model,
        kernel.reshape(PAIRS * COMPS, WIDTH, WIDTH),
        tile_index,
        station_of,
        line_length,
    )
    return grad_model, walk.reshape(COMPS, LINES, STEPS)


def solution(mesh):
    in_specs = (
        P(None, "tile", "tm"),
        P(None, "tile", "tm"),
        P(("tm", "tile"), None),
        P(("tm", "tile"), None, None, None, None),
        P(("tm", "tile"), None),
        P("tile", "tm"),
        P("tile"),
    )
    out_specs = (P(("tm", "tile"), None), P(None, "tile", "tm"))
    return jax.shard_map(shards, mesh=mesh, in_specs=in_specs, out_specs=out_specs, check_vma=False)
```

```python
import functools
import math

import jax
import jax.numpy as jnp
from jax import lax
from jax.experimental import pallas as pl
from jax.experimental.pallas import tpu as pltpu
from jax.sharding import PartitionSpec as P

MESH = pl.DeviceIdType.MESH
BF = jnp.bfloat16
F32 = jnp.float32
I32 = jnp.int32
TM = 16
TILE = 8
DEV = TM * TILE
CAP = 32
SLOT = 16
COMPS = 9
CHUNK = 64
LANE_COMPS = 6
LINES = 8
STEPS = 512
WIDTH = 256
HALF = 128
NNZ = 4
PAIRS = 8
LABEL = 9
LINE = 10
SPARE = 12
GRID = sorted(((x, y) for x in range(4) for y in range(4)), key=lambda o: -sum(min(v, 4 - v) for v in o))
COLUMNS = (4, 5, 3, 2, 6, 7, 1, 0)


def iota(shape, dim):
    return lax.broadcasted_iota(I32, shape, dim)


def nn(a, b):
    return lax.dot_general(a, b, (((1,), (0,)), ((), ())), preferred_element_type=F32)


def nt(a, b):
    return lax.dot_general(a, b, (((1,), (1,)), ((), ())), preferred_element_type=F32)


def split(x, count):
    pieces = []
    for _ in range(count):
        top = x.astype(BF).astype(F32)
        pieces.append(top)
        x = x - top
    return pieces


def ones(mask):
    return jnp.where(mask, 1.0, 0.0).astype(BF)


def spare_lane(line, comp):
    return (line * 4 + comp // 4) * SLOT + SPARE + comp % 4


def body(
    obs_hbm, inc_hbm, model_hbm, kern_ref, index_hbm, station_hbm, length_hbm,
    grad_hbm, walk_hbm,
    grad_ref, obs_ref, inc_ref, model_ref, index_ref, station_ref, length_ref,
    kern_v, hot_v, spread_v, rank_v, off_v, stage_v, table_v, early_v, cell_v, pred_v, adj_v, wide_v, res_v, fold_v,
    mod_out, mod_in, out1, in1, out2, in2, out3, in3,
    load_sem, save_sem, kern_sem, local_sem, send_sem, recv_sem,
):
    tm, tile = lax.axis_index("tm"), lax.axis_index("tile")
    me = tm * TILE + tile
    tiles = [lax.rem(tile + k, TILE) for k in COLUMNS]

    loads = [
        pltpu.make_async_copy(hbm, ref, load_sem.at[i])
        for i, (hbm, ref) in enumerate(
            (
                (inc_hbm, inc_ref), (obs_hbm, obs_ref), (model_hbm, model_ref),
                (station_hbm, station_ref), (length_hbm, length_ref), (index_hbm, index_ref),
            )
        )
    ]
    for load in loads:
        load.start()
    barrier = pltpu.get_barrier_semaphore()

    def greet(row, columns):
        for t in columns:
            pl.semaphore_signal(barrier, inc=1, device_id=(row, t), device_id_type=MESH)

    greet(tm, tiles[:-1])

    def greet_row(i, _):
        greet(lax.rem(tm + i, TM), tiles)
        return 0

    lax.fori_loop(1, TM, greet_row, 0)
    fetch = pltpu.make_async_copy(kern_ref, kern_v, kern_sem)
    fetch.start()

    def send_all(src_of, dst, slot):
        own = pltpu.make_async_copy(src_of(me), dst.at[me], local_sem.at[slot])
        own.start()
        for dx, dy in GRID:
            row = lax.rem(tm // 4 + dx, 4) * 4 + lax.rem(lax.rem(tm, 4) + dy, 4)
            for k, t in zip(COLUMNS, tiles):
                if (dx, dy, k) != (0, 0, 0):
                    pltpu.make_async_remote_copy(
                        src_ref=src_of(row * TILE + t), dst_ref=dst.at[me],
                        send_sem=send_sem.at[slot], recv_sem=recv_sem.at[slot],
                        device_id=(row, t), device_id_type=MESH,
                    ).start()
        return own

    def all_arrived(dst, slot, own):
        own.wait()
        span = dst.at[pl.ds(0, DEV - 1)]
        pltpu.make_async_copy(span, span, recv_sem.at[slot]).wait()

    def all_sent(dst, slot):
        span = dst.at[pl.ds(0, DEV - 1)]
        pltpu.make_async_copy(span, span, send_sem.at[slot]).wait()

    for load in loads:
        load.wait()
    cells = model_ref[...]
    mod_out[...] = jnp.concatenate([cells[:, :HALF], cells[:, HALF:]], axis=0).astype(BF)

    upto = ones(iota((WIDTH, WIDTH), 0) <= iota((WIDTH, WIDTH), 1))
    steps = inc_ref[...]
    rows = COMPS * LINES
    first = jnp.concatenate(split(steps[:, :WIDTH], 3), axis=0).astype(BF)
    second = jnp.concatenate(split(steps[:, WIDTH:], 3), axis=0).astype(BF)
    first, second = nn(first, upto), nn(second, upto)
    first = first[:rows] + first[rows : 2 * rows] + first[2 * rows :]
    second = second[:rows] + second[rows : 2 * rows] + second[2 * rows :]
    second = second + first[:, WIDTH - 1 :]
    totals = second[:, WIDTH - 1 :]
    first = first - obs_ref[:, :WIDTH]
    second = second - obs_ref[:, WIDTH:]
    for j, part in enumerate((first[:, :HALF], first[:, HALF:], second[:, :HALF], second[:, HALF:])):
        off_v[pl.ds(j * DEV, rows), :] = part
        off_v[pl.ds(j * DEV + rows, DEV - rows), :] = jnp.zeros((DEV - rows, HALF), F32)

    def one_line(l, base):
        lanes = pl.ds(pl.multiple_of(l * STEPS, STEPS), STEPS)
        station = station_ref[pl.ds(l, 1), :]
        owner = station // WIDTH
        inner = station % WIDTH
        line_place = (owner % 2) * HALF + owner // 2
        hit = iota((WIDTH, STEPS), 0) == line_place
        hot = ones(hit)
        hot_v[:, lanes] = hot
        ranks = []
        for h in range(2):
            part = slice(h * WIDTH, (h + 1) * WIDTH)
            count = nn(hot[:, part], upto)
            ranks.append(jnp.sum(jnp.where(hit[:, part], count + base, 0.0), axis=0, keepdims=True))
            base = base + count[:, WIDTH - 1 :]
        rank = jnp.concatenate(ranks, axis=1) - 1.0
        rank_v[pl.ds(l, 1), :] = rank
        position = tm * STEPS + iota((1, STEPS), 1)
        label = jnp.where(position < length_ref[l], inner + 1, 0).astype(F32)
        comp = iota((SLOT, STEPS), 0)
        values = jnp.concatenate([off_v[pl.ds(j * DEV + l, SLOT, stride=LINES), :] for j in range(4)], axis=1)
        values = jnp.where(comp == LABEL, label, values)
        values = jnp.where(comp == LINE, l.astype(F32), values)
        for r in range(CAP):
            spread_v[pl.ds(r * SLOT, SLOT), lanes] = jnp.where(rank == float(r), values, 0.0).astype(BF)
        return base

    lax.fori_loop(0, LINES, one_line, jnp.zeros((WIDTH, 1), F32))

    placed = nt(hot_v[...], spread_v[...])
    row = iota((rows, CAP * SLOT), 0)
    at_spare = iota((rows, CAP * SLOT), 1) == spare_lane(row % LINES, row // LINES)
    for s, part in enumerate(split(totals, 2)):
        extra = jnp.sum(jnp.where(at_spare, part, 0.0), axis=0, keepdims=True)
        half = placed[s * HALF : (s + 1) * HALF] + extra
        for g in range(4):
            stage_v[pl.ds(s * 4 + g, DEV, stride=8), :] = half[:, g * HALF : (g + 1) * HALF]

    def pack(dst):
        dst[...] = stage_v[...].reshape(DEV, 8, HALF).astype(BF)

    def unpack(src):
        stage_v[...] = src[...].astype(F32).reshape(DEV * 8, HALF)

    pack(out1)
    pl.semaphore_wait(barrier, DEV - 1)
    own_mod = send_all(lambda p: mod_out, mod_in, 0)
    own1 = send_all(lambda p: out1.at[p], in1, 1)

    fetch.wait()
    all_arrived(mod_in, 0, own_mod)
    pair_row = iota((SLOT, DEV * 8), 0)
    pair_lane = iota((SLOT, DEV * 8), 1)
    base_row = jnp.full((SLOT, DEV * 8), -8, I32)
    for q in range(PAIRS):
        cell = index_ref[q // NNZ, q % NNZ]
        base_row = jnp.where(pair_row == q, (cell // 4) * 8 + cell % 4, base_row)
    every = mod_in[...].reshape(DEV * 8, HALF)
    chosen = jnp.concatenate([nn(ones(pair_lane == base_row + 4 * h), every) for h in range(2)], axis=1)
    cell_v[...] = chosen
    comp_row = iota((SLOT, HALF), 0)
    wide_row = iota((SLOT, WIDTH), 0)
    for s in range(2):
        vectors = [cell_v[pl.ds(s * NNZ + k, 1), :] for k in range(NNZ)]

        def forward(i, state):
            halves, across = list(state[:2]), state[2]
            last = LANE_COMPS + i
            for c in (2 * i, 2 * i + 1):
                sums = []
                for j in range(0, WIDTH, CHUNK):
                    total = jnp.zeros((CHUNK, HALF), F32)
                    for k in range(NNZ):
                        block = kern_v[(s * NNZ + k) * COMPS + c, pl.ds(j, CHUNK), :].astype(F32) * vectors[k]
                        total = total + block[:, :HALF] + block[:, HALF:]
                    sums.append(total)
                for h in range(2):
                    tall = jnp.concatenate(sums[h * HALF // CHUNK : (h + 1) * HALF // CHUNK], axis=0).T
                    halves[h] = jnp.where(comp_row == c, jnp.sum(tall, axis=0, keepdims=True), halves[h])
            for k in range(NNZ):
                left = jnp.where(wide_row == last, vectors[k], 0.0).astype(BF)
                across = across + nt(left, kern_v[(s * NNZ + k) * COMPS + last])
            return (*halves, across)

        state = lax.fori_loop(
            0, LANE_COMPS // 2, forward, (*[jnp.zeros((SLOT, HALF), F32)] * 2, jnp.zeros((SLOT, WIDTH), F32))
        )
        for h in range(2):
            part = slice(h * HALF, (h + 1) * HALF)
            pred_v[s, :, pl.ds(h * HALF, HALF)] = state[h] + state[2][:, part]

    all_arrived(in1, 1, own1)
    unpack(in1)
    for s in range(2):
        for g in range(4):
            table_v[s, pl.ds(g * HALF, HALF), :] = stage_v[pl.ds(s * 4 + g, DEV, stride=8), :].T
    q_row = iota((DEV, CAP * SLOT), 0)
    pick = ones(
        (iota((DEV, CAP * SLOT), 1) == spare_lane(q_row // SLOT, q_row % SLOT)) & (q_row % SLOT < COMPS)
    )
    q_lane = iota((CAP * SLOT, DEV), 1)
    put = ones(
        (iota((CAP * SLOT, DEV), 0) == spare_lane(q_lane // SLOT, q_lane % SLOT)) & (q_lane % SLOT < COMPS)
    )
    source, target = iota((DEV, DEV), 0), iota((DEV, DEV), 1)
    same_lines = source % TILE == target % TILE
    before = ones(same_lines & (source // TILE < target // TILE))
    after = ones(same_lines & (source // TILE > target // TILE))
    early = jnp.zeros((DEV, DEV), F32)
    for s in range(2):
        part = nn(pick, table_v[s].astype(BF))
        early = early + nn(part.astype(BF), before)
    early_v[...] = early

    lane_count = 2 * HALF
    slot_row = iota((SLOT, lane_count), 0)
    station_row = iota((WIDTH, lane_count), 0)
    tables = [[pred_v[s, :, pl.ds(h * HALF, HALF)] for h in range(2)] for s in range(2)]

    def slots(i, carry):
        totals = list(carry[:2])
        lines = list(carry[2:])
        start = pl.multiple_of(i * 2 * SLOT, 2 * SLOT)
        for s in range(2):
            pair = [table_v[s, pl.ds(start + j * SLOT, SLOT), :] for j in range(2)]
            got = jnp.concatenate(pair, axis=1)
            label = got[LABEL : LABEL + 1]
            line = got[LINE : LINE + 1]
            match = ones(station_row == label.astype(I32) - 1)
            picked = []
            for part in pair:
                at = jnp.broadcast_to(jnp.maximum(part[LABEL : LABEL + 1].astype(I32) - 1, 0), (SLOT, HALF))
                lane = at % HALF
                low = jnp.take_along_axis(tables[s][0], lane, axis=1)
                high = jnp.take_along_axis(tables[s][1], lane, axis=1)
                picked.append(jnp.where(at >= HALF, high, low))
            value = jnp.concatenate(picked, axis=1) + got
            for l in range(LINES):
                walk = early_v[pl.ds(l * SLOT, SLOT), :]
                value = value + jnp.where(line == float(l), jnp.concatenate([walk, walk], axis=1), 0.0)
            value = jnp.where((label > 0.0) & (slot_row < COMPS), value, 0.0)
            res_v[s, pl.ds(start, SLOT), :] = value[:, :HALF]
            res_v[s, pl.ds(start + SLOT, SLOT), :] = value[:, HALF:]
            for l in range(LINES):
                mine = jnp.where(line == float(l), value, 0.0)
                lines[l] = lines[l] + mine[:, :HALF] + mine[:, HALF:]
            totals[s] = totals[s] + nt(jnp.concatenate(split(value, 3), axis=0).astype(BF), match)
        return (*totals, *lines)

    carry = lax.fori_loop(
        0, CAP // 2, slots,
        (*[jnp.zeros((3 * SLOT, WIDTH), F32)] * 2, *[jnp.zeros((SLOT, HALF), F32)] * LINES),
    )
    sums = [total[:SLOT] + total[SLOT : 2 * SLOT] + total[2 * SLOT :] for total in carry[:2]]
    line_sums = list(carry[2:])

    gathered = jnp.concatenate(line_sums, axis=0)
    three = nn(jnp.concatenate(split(gathered, 3), axis=0).astype(BF), after)
    beyond = three[:DEV] + three[DEV : 2 * DEV] + three[2 * DEV :]
    for s, part in enumerate(split(beyond, 2)):
        full = res_v[s] + nn(put, part.astype(BF))
        for g in range(4):
            stage_v[pl.ds(s * 4 + g, DEV, stride=8), :] = full[g * HALF : (g + 1) * HALF, :].T
    pack(out2)
    own2 = send_all(lambda p: out2.at[p], in2, 2)

    gain = 1.0 / math.sqrt(LINES * TILE * STEPS * TM / (2 * DEV * WIDTH))
    filler = jnp.zeros((HALF - SLOT, WIDTH), F32)
    contributions = []
    across = jnp.zeros((SLOT, WIDTH), F32)
    for s in range(2):
        sheet = (sums[s] * gain).astype(BF).astype(F32)
        tall = jnp.concatenate([sheet, filler], axis=0)
        adj_v[s] = jnp.concatenate([tall[:, :HALF].T, tall[:, HALF:].T], axis=0)

        def adjoint(i, state):
            totals, across = list(state[:NNZ]), state[NNZ]
            start = pl.multiple_of(i * CHUNK, CHUNK)
            weights = adj_v[s, pl.ds(start, CHUNK), :]
            for c in range(LANE_COMPS):
                weight = jnp.broadcast_to(weights[:, c : c + 1], (CHUNK, WIDTH))
                for k in range(NNZ):
                    block = kern_v[(s * NNZ + k) * COMPS + c, pl.ds(start, CHUNK), :].astype(F32) * weight
                    totals[k] = totals[k] + jnp.sum(block.reshape(CHUNK // 8, 8, WIDTH), axis=0)
            for c in range(LANE_COMPS, COMPS):
                left = jnp.where(wide_row == s * NNZ + i, sheet[c : c + 1], 0.0).astype(BF)
                across = across + nn(left, kern_v[(s * NNZ + i) * COMPS + c])
            return (*totals, across)

        state = lax.fori_loop(0, NNZ, adjoint, (*[jnp.zeros((8, WIDTH), F32)] * NNZ, across))
        contributions += [jnp.sum(total, axis=0, keepdims=True) for total in state[:NNZ]]
        across = state[NNZ]
    contributions = jnp.concatenate(contributions, axis=0) + across[:PAIRS]
    pieces = split(contributions, 2)
    stack = [piece[:, h * HALF : (h + 1) * HALF] for h in range(2) for piece in pieces]
    stack = jnp.concatenate(stack + [jnp.zeros((HALF - 4 * PAIRS, HALF), F32)], axis=0).astype(BF)
    lane = iota((1, HALF), 1)
    goal = jnp.full((1, HALF), -8, I32)
    for q in range(PAIRS):
        cell = index_ref[q // NNZ, q % NNZ]
        goal = jnp.where(lane % PAIRS == q, (cell // 4) * 8 + cell % 4, goal)
    goal = jnp.where(lane < 4 * PAIRS, goal + 4 * (lane // (2 * PAIRS)), -8)
    stage_v[...] = nn(ones(iota((DEV * 8, HALF), 0) == goal), stack)
    pack(out3)
    own3 = send_all(lambda p: out3.at[p], in3, 3)

    all_arrived(in2, 2, own2)
    unpack(in2)
    for s in range(2):
        for g in range(4):
            wide_v[pl.ds(g * HALF, HALF), pl.ds(s * HALF, HALF)] = (
                stage_v[pl.ds(s * 4 + g, DEV, stride=8), :].T.astype(BF)
            )
    rest = jnp.sum(nn(pick, wide_v[...]), axis=1, keepdims=True)

    def collect(l, _):
        lanes = pl.ds(pl.multiple_of(l * STEPS, STEPS), STEPS)
        every = nn(wide_v[...], hot_v[:, lanes])
        rank = rank_v[pl.ds(l, 1), :]
        value = jnp.zeros((SLOT, STEPS), F32)
        for r in range(CAP):
            value = value + jnp.where(rank == float(r), every[r * SLOT : (r + 1) * SLOT], 0.0)
        fold_v[pl.ds(pl.multiple_of(l * SLOT, SLOT), SLOT), :] = value
        return 0

    lax.fori_loop(0, LINES, collect, 0)
    onward = ones(iota((WIDTH, WIDTH), 0) >= iota((WIDTH, WIDTH), 1))
    late = nn(fold_v[:, WIDTH:].astype(BF), onward) + rest
    soon = nn(fold_v[:, :WIDTH].astype(BF), onward) + late[:, :1]
    scale = 1.0 / math.sqrt(STEPS * TM)
    saves = []
    for j, part in enumerate((soon[:, :HALF], soon[:, HALF:], late[:, :HALF], late[:, HALF:])):
        for l in range(LINES):
            off_v[pl.ds(j * DEV + l, SLOT, stride=LINES), :] = part[l * SLOT : (l + 1) * SLOT] * scale
        save = pltpu.make_async_copy(
            off_v.at[pl.ds(j * DEV, rows)], walk_hbm.at[:, pl.ds(j * HALF, HALF)], save_sem.at[j]
        )
        save.start()
        saves.append(save)

    all_arrived(in3, 3, own3)
    grad = jnp.sum(in3[...].astype(F32), axis=0)
    grad_ref[...] = jnp.concatenate([grad[:4], grad[4:]], axis=1)
    save = pltpu.make_async_copy(grad_ref, grad_hbm, save_sem.at[4])
    save.start()
    for save in saves + [save]:
        save.wait()
    for slot, dst in enumerate((mod_in, in1, in2, in3)):
        all_sent(dst, slot)


def deliver(grad_in, walk_in, grad_out, walk_out):
    walk_out[...] = walk_in[...]
    grad_out[...] = grad_in[...]


def shards(observed, increments, model, kernel, tile_index, station_of, line_length):
    rows = COMPS * LINES
    anywhere = pl.BlockSpec(memory_space=pl.ANY)
    message = pltpu.VMEM((DEV, 8, HALF), BF)
    grad_model, walk = pl.pallas_call(
        body,
        out_shape=(
            jax.ShapeDtypeStruct((4, WIDTH), F32),
            jax.ShapeDtypeStruct((rows, STEPS), F32),
        ),
        in_specs=[anywhere] * 7,
        out_specs=(anywhere, anywhere),
        scratch_shapes=[
            pltpu.VMEM((4, WIDTH), F32),
            pltpu.VMEM((rows, STEPS), F32),
            pltpu.VMEM((rows, STEPS), F32),
            pltpu.VMEM((4, WIDTH), F32),
            pltpu.SMEM((2, NNZ), I32),
            pltpu.VMEM((LINES, STEPS), I32),
            pltpu.SMEM((LINES,), I32),
            pltpu.VMEM((PAIRS * COMPS, WIDTH, WIDTH), BF),
            pltpu.VMEM((WIDTH, LINES * STEPS), BF),
            pltpu.VMEM((CAP * SLOT, LINES * STEPS), BF),
            pltpu.VMEM((LINES, STEPS), F32),
            pltpu.VMEM((4 * DEV, HALF), F32),
            pltpu.VMEM((DEV * 8, HALF), F32),
            pltpu.VMEM((2, CAP * SLOT, HALF), F32),
            pltpu.VMEM((DEV, DEV), F32),
            pltpu.VMEM((SLOT, WIDTH), F32),
            pltpu.VMEM((2, SLOT, WIDTH), F32),
            pltpu.VMEM((2, WIDTH, HALF), F32),
            pltpu.VMEM((CAP * SLOT, WIDTH), BF),
            pltpu.VMEM((2, CAP * SLOT, HALF), F32),
            pltpu.VMEM((DEV, STEPS), F32),
            pltpu.VMEM((8, HALF), BF),
            message, message, message, message, message, message, message,
            pltpu.SemaphoreType.DMA((6,)),
            pltpu.SemaphoreType.DMA((5,)),
            pltpu.SemaphoreType.DMA,
            pltpu.SemaphoreType.DMA((4,)),
            pltpu.SemaphoreType.DMA((4,)),
            pltpu.SemaphoreType.DMA((4,)),
        ],
        compiler_params=pltpu.CompilerParams(
            collective_id=0, has_side_effects=True, vmem_limit_bytes=60 * 1024 * 1024
        ),
        name="invert",
    )(
        observed.reshape(rows, STEPS),
        increments.reshape(rows, STEPS),
        model,
        kernel.reshape(PAIRS * COMPS, WIDTH, WIDTH),
        tile_index,
        station_of,
        line_length,
    )
    grad_model, walk = pl.pallas_call(
        deliver,
        out_shape=(
            jax.ShapeDtypeStruct((4, WIDTH), F32),
            jax.ShapeDtypeStruct((rows, STEPS), F32),
        ),
        name="deliver",
    )(grad_model, walk)
    return grad_model, walk.reshape(COMPS, LINES, STEPS)


def solution(mesh):
    in_specs = (
        P(None, "tile", "tm"),
        P(None, "tile", "tm"),
        P(("tm", "tile"), None),
        P(("tm", "tile"), None, None, None, None),
        P(("tm", "tile"), None),
        P("tile", "tm"),
        P("tile"),
    )
    out_specs = (P(("tm", "tile"), None), P(None, "tile", "tm"))
    return jax.shard_map(shards, mesh=mesh, in_specs=in_specs, out_specs=out_specs, check_vma=False)
```

```python
import functools
import math

import jax
import jax.numpy as jnp
from jax import lax
from jax.experimental import pallas as pl
from jax.experimental.pallas import tpu as pltpu
from jax.sharding import PartitionSpec as P

MESH = pl.DeviceIdType.MESH
BF = jnp.bfloat16
F32 = jnp.float32
I32 = jnp.int32
TM = 16
TILE = 8
DEV = TM * TILE
CAP = 32
SLOT = 16
COMPS = 9
CHUNK = 64
LANE_COMPS = 6
LINES = 8
STEPS = 512
WIDTH = 256
HALF = 128
NNZ = 4
PAIRS = 8
LABEL = 9
LINE = 10
SPARE = 12
GRID = sorted(((x, y) for x in range(4) for y in range(4)), key=lambda o: -sum(min(v, 4 - v) for v in o))
COLUMNS = (4, 5, 3, 2, 6, 7, 1, 0)


def iota(shape, dim):
    return lax.broadcasted_iota(I32, shape, dim)


def nn(a, b):
    return lax.dot_general(a, b, (((1,), (0,)), ((), ())), preferred_element_type=F32)


def nt(a, b):
    return lax.dot_general(a, b, (((1,), (1,)), ((), ())), preferred_element_type=F32)


def split(x, count):
    pieces = []
    for _ in range(count):
        top = x.astype(BF).astype(F32)
        pieces.append(top)
        x = x - top
    return pieces


def ones(mask):
    return jnp.where(mask, 1.0, 0.0).astype(BF)


def spare_lane(line, comp):
    return (line * 4 + comp // 4) * SLOT + SPARE + comp % 4


def body(
    obs_hbm, inc_hbm, model_hbm, kern_ref, index_hbm, station_hbm, length_hbm,
    grad_hbm, walk_hbm,
    grad_ref, obs_ref, inc_ref, model_ref, index_ref, station_ref, length_ref,
    kern_v, hot_v, spread_v, rank_v, off_v, pick_v, put_v, before_v, after_v, goal_v, onward_v, stage_v, placed_v, table_v, early_v, cell_v, pred_v, adj_v, wide_v, res_v, fold_v,
    mod_out, mod_in, out1, in1, out2, in2, out3, in3,
    load_sem, save_sem, kern_sem, local_sem, send_sem, recv_sem,
):
    tm, tile = lax.axis_index("tm"), lax.axis_index("tile")
    me = tm * TILE + tile
    tiles = [lax.rem(tile + k, TILE) for k in COLUMNS]

    loads = [
        pltpu.make_async_copy(hbm, ref, load_sem.at[i])
        for i, (hbm, ref) in enumerate(
            (
                (inc_hbm, inc_ref), (obs_hbm, obs_ref), (model_hbm, model_ref),
                (station_hbm, station_ref), (length_hbm, length_ref), (index_hbm, index_ref),
            )
        )
    ]
    for load in loads:
        load.start()
    barrier = pltpu.get_barrier_semaphore()

    def greet(row, columns):
        for t in columns:
            pl.semaphore_signal(barrier, inc=1, device_id=(row, t), device_id_type=MESH)

    greet(tm, tiles[:-1])

    def greet_row(i, _):
        greet(lax.rem(tm + i, TM), tiles)
        return 0

    lax.fori_loop(1, TM, greet_row, 0)
    fetch = pltpu.make_async_copy(kern_ref, kern_v, kern_sem)
    fetch.start()

    def send_all(src_of, dst, slot):
        own = pltpu.make_async_copy(src_of(me), dst.at[me], local_sem.at[slot])
        own.start()
        for dx, dy in GRID:
            row = lax.rem(tm // 4 + dx, 4) * 4 + lax.rem(lax.rem(tm, 4) + dy, 4)
            for k, t in zip(COLUMNS, tiles):
                if (dx, dy, k) != (0, 0, 0):
                    pltpu.make_async_remote_copy(
                        src_ref=src_of(row * TILE + t), dst_ref=dst.at[me],
                        send_sem=send_sem.at[slot], recv_sem=recv_sem.at[slot],
                        device_id=(row, t), device_id_type=MESH,
                    ).start()
        return own

    def all_arrived(dst, slot, own):
        own.wait()
        span = dst.at[pl.ds(0, DEV - 1)]
        pltpu.make_async_copy(span, span, recv_sem.at[slot]).wait()

    def all_sent(dst, slot):
        span = dst.at[pl.ds(0, DEV - 1)]
        pltpu.make_async_copy(span, span, send_sem.at[slot]).wait()

    for load in loads:
        load.wait()
    cells = model_ref[...]
    mod_out[...] = jnp.concatenate([cells[:, :HALF], cells[:, HALF:]], axis=0).astype(BF)

    upto = ones(iota((WIDTH, WIDTH), 0) <= iota((WIDTH, WIDTH), 1))
    steps = inc_ref[...]
    rows = COMPS * LINES
    first = jnp.concatenate(split(steps[:, :WIDTH], 3), axis=0).astype(BF)
    second = jnp.concatenate(split(steps[:, WIDTH:], 3), axis=0).astype(BF)
    first, second = nn(first, upto), nn(second, upto)
    first = first[:rows] + first[rows : 2 * rows] + first[2 * rows :]
    second = second[:rows] + second[rows : 2 * rows] + second[2 * rows :]
    second = second + first[:, WIDTH - 1 :]
    totals = second[:, WIDTH - 1 :]
    first = first - obs_ref[:, :WIDTH]
    second = second - obs_ref[:, WIDTH:]
    for j, part in enumerate((first[:, :HALF], first[:, HALF:], second[:, :HALF], second[:, HALF:])):
        off_v[pl.ds(j * DEV, rows), :] = part
        off_v[pl.ds(j * DEV + rows, DEV - rows), :] = jnp.zeros((DEV - rows, HALF), F32)

    def one_line(l, base):
        lanes = pl.ds(l * STEPS, STEPS)
        station = station_ref[pl.ds(l, 1), :]
        owner = station // WIDTH
        inner = station % WIDTH
        line_place = (owner % 2) * HALF + owner // 2
        hit = iota((WIDTH, STEPS), 0) == line_place
        hot = ones(hit)
        hot_v[:, lanes] = hot
        ranks = []
        for h in range(2):
            part = slice(h * WIDTH, (h + 1) * WIDTH)
            count = nn(hot[:, part], upto)
            ranks.append(jnp.sum(jnp.where(hit[:, part], count + base, 0.0), axis=0, keepdims=True))
            base = base + count[:, WIDTH - 1 :]
        rank = jnp.concatenate(ranks, axis=1) - 1.0
        rank_v[pl.ds(l, 1), :] = rank
        position = tm * STEPS + iota((1, STEPS), 1)
        label = jnp.where(position < length_ref[l], inner + 1, 0).astype(F32)
        comp = iota((SLOT, STEPS), 0)
        values = jnp.concatenate([off_v[pl.ds(j * DEV + l, SLOT, stride=LINES), :] for j in range(4)], axis=1)
        values = jnp.where(comp == LABEL, label, values)
        values = jnp.where(comp == LINE, float(l), values)
        for r in range(CAP):
            spread_v[pl.ds(r * SLOT, SLOT), lanes] = jnp.where(rank == float(r), values, 0.0).astype(BF)
        return base

    def place(l):
        lanes = pl.ds(l * STEPS, STEPS)
        fresh = nt(hot_v[:, lanes], spread_v[:, lanes])
        placed_v[...] = fresh if l == 0 else placed_v[...] + fresh

    base = jnp.zeros((WIDTH, 1), F32)
    for l in range(LINES):
        base = one_line(l, base)
        if l:
            place(l - 1)
    place(LINES - 1)
    row = iota((rows, CAP * SLOT), 0)
    at_spare = iota((rows, CAP * SLOT), 1) == spare_lane(row % LINES, row // LINES)
    for s, part in enumerate(split(totals, 2)):
        extra = jnp.sum(jnp.where(at_spare, part, 0.0), axis=0, keepdims=True)
        half = placed_v[pl.ds(s * HALF, HALF), :] + extra
        for g in range(4):
            stage_v[pl.ds(s * 4 + g, DEV, stride=8), :] = half[:, g * HALF : (g + 1) * HALF]

    def pack(dst):
        dst[...] = stage_v[...].reshape(DEV, 8, HALF).astype(BF)

    def unpack(src):
        stage_v[...] = src[...].astype(F32).reshape(DEV * 8, HALF)

    pack(out1)
    pl.semaphore_wait(barrier, DEV - 1)
    own_mod = send_all(lambda p: mod_out, mod_in, 0)
    own1 = send_all(lambda p: out1.at[p], in1, 1)

    q_row = iota((DEV, CAP * SLOT), 0)
    pick_v[...] = ones(
        (iota((DEV, CAP * SLOT), 1) == spare_lane(q_row // SLOT, q_row % SLOT)) & (q_row % SLOT < COMPS)
    )
    q_lane = iota((CAP * SLOT, DEV), 1)
    put_v[...] = ones(
        (iota((CAP * SLOT, DEV), 0) == spare_lane(q_lane // SLOT, q_lane % SLOT)) & (q_lane % SLOT < COMPS)
    )
    source, target = iota((DEV, DEV), 0), iota((DEV, DEV), 1)
    same_lines = source % TILE == target % TILE
    before_v[...] = ones(same_lines & (source // TILE < target // TILE))
    after_v[...] = ones(same_lines & (source // TILE > target // TILE))
    lane = iota((1, HALF), 1)
    goal = jnp.full((1, HALF), -8, I32)
    for q in range(PAIRS):
        cell = index_ref[q // NNZ, q % NNZ]
        goal = jnp.where(lane % PAIRS == q, (cell // 4) * 8 + cell % 4, goal)
    goal = jnp.where(lane < 4 * PAIRS, goal + 4 * (lane // (2 * PAIRS)), -8)
    goal_v[...] = ones(iota((DEV * 8, HALF), 0) == goal)
    onward_v[...] = ones(iota((WIDTH, WIDTH), 0) >= iota((WIDTH, WIDTH), 1))
    fetch.wait()
    all_arrived(mod_in, 0, own_mod)
    pair_row = iota((SLOT, DEV * 8), 0)
    pair_lane = iota((SLOT, DEV * 8), 1)
    base_row = jnp.full((SLOT, DEV * 8), -8, I32)
    for q in range(PAIRS):
        cell = index_ref[q // NNZ, q % NNZ]
        base_row = jnp.where(pair_row == q, (cell // 4) * 8 + cell % 4, base_row)
    every = mod_in[...].reshape(DEV * 8, HALF)
    chosen = jnp.concatenate([nn(ones(pair_lane == base_row + 4 * h), every) for h in range(2)], axis=1)
    cell_v[...] = chosen
    comp_row = iota((SLOT, HALF), 0)
    wide_row = iota((SLOT, WIDTH), 0)
    for s in range(2):
        vectors = [cell_v[pl.ds(s * NNZ + k, 1), :] for k in range(NNZ)]

        def forward(i, state):
            halves, across = list(state[:2]), state[2]
            last = LANE_COMPS + i
            for c in (2 * i, 2 * i + 1):
                sums = []
                for j in range(0, WIDTH, CHUNK):
                    total = jnp.zeros((CHUNK, HALF), F32)
                    for k in range(NNZ):
                        block = kern_v[(s * NNZ + k) * COMPS + c, pl.ds(j, CHUNK), :].astype(F32) * vectors[k]
                        total = total + block[:, :HALF] + block[:, HALF:]
                    sums.append(total)
                for h in range(2):
                    tall = jnp.concatenate(sums[h * HALF // CHUNK : (h + 1) * HALF // CHUNK], axis=0).T
                    halves[h] = jnp.where(comp_row == c, jnp.sum(tall, axis=0, keepdims=True), halves[h])
            for k in range(NNZ):
                left = jnp.where(wide_row == last, vectors[k], 0.0).astype(BF)
                across = across + nt(left, kern_v[(s * NNZ + k) * COMPS + last])
            return (*halves, across)

        state = lax.fori_loop(
            0, LANE_COMPS // 2, forward, (*[jnp.zeros((SLOT, HALF), F32)] * 2, jnp.zeros((SLOT, WIDTH), F32))
        )
        for h in range(2):
            part = slice(h * HALF, (h + 1) * HALF)
            pred_v[s, :, pl.ds(h * HALF, HALF)] = state[h] + state[2][:, part]

    all_arrived(in1, 1, own1)
    unpack(in1)
    for s in range(2):
        for g in range(4):
            table_v[s, pl.ds(g * HALF, HALF), :] = stage_v[pl.ds(s * 4 + g, DEV, stride=8), :].T
    early = jnp.zeros((DEV, DEV), F32)
    for s in range(2):
        part = nn(pick_v[...], table_v[s].astype(BF))
        early = early + nn(part.astype(BF), before_v[...])
    early_v[...] = early

    lane_count = 2 * HALF
    slot_row = iota((SLOT, lane_count), 0)
    station_row = iota((WIDTH, lane_count), 0)
    tables = [[pred_v[s, :, pl.ds(h * HALF, HALF)] for h in range(2)] for s in range(2)]

    def slots(i, carry):
        totals = list(carry[:2])
        lines = list(carry[2:])
        start = pl.multiple_of(i * 2 * SLOT, 2 * SLOT)
        for s in range(2):
            pair = [table_v[s, pl.ds(start + j * SLOT, SLOT), :] for j in range(2)]
            got = jnp.concatenate(pair, axis=1)
            label = got[LABEL : LABEL + 1]
            line = got[LINE : LINE + 1]
            match = ones(station_row == label.astype(I32) - 1)
            picked = []
            for part in pair:
                at = jnp.broadcast_to(jnp.maximum(part[LABEL : LABEL + 1].astype(I32) - 1, 0), (SLOT, HALF))
                lane = at % HALF
                low = jnp.take_along_axis(tables[s][0], lane, axis=1)
                high = jnp.take_along_axis(tables[s][1], lane, axis=1)
                picked.append(jnp.where(at >= HALF, high, low))
            value = jnp.concatenate(picked, axis=1) + got
            for l in range(LINES):
                walk = early_v[pl.ds(l * SLOT, SLOT), :]
                value = value + jnp.where(line == float(l), jnp.concatenate([walk, walk], axis=1), 0.0)
            value = jnp.where((label > 0.0) & (slot_row < COMPS), value, 0.0)
            res_v[s, pl.ds(start, SLOT), :] = value[:, :HALF]
            res_v[s, pl.ds(start + SLOT, SLOT), :] = value[:, HALF:]
            for l in range(LINES):
                mine = jnp.where(line == float(l), value, 0.0)
                lines[l] = lines[l] + mine[:, :HALF] + mine[:, HALF:]
            totals[s] = totals[s] + nt(jnp.concatenate(split(value, 3), axis=0).astype(BF), match)
        return (*totals, *lines)

    carry = lax.fori_loop(
        0, CAP // 2, slots, unroll=2, init_val=
        (*[jnp.zeros((3 * SLOT, WIDTH), F32)] * 2, *[jnp.zeros((SLOT, HALF), F32)] * LINES),
    )
    sums = [total[:SLOT] + total[SLOT : 2 * SLOT] + total[2 * SLOT :] for total in carry[:2]]
    line_sums = list(carry[2:])

    gathered = jnp.concatenate(line_sums, axis=0)
    three = nn(jnp.concatenate(split(gathered, 3), axis=0).astype(BF), after_v[...])
    beyond = three[:DEV] + three[DEV : 2 * DEV] + three[2 * DEV :]
    for s, part in enumerate(split(beyond, 2)):
        full = res_v[s] + nn(put_v[...], part.astype(BF))
        for g in range(4):
            stage_v[pl.ds(s * 4 + g, DEV, stride=8), :] = full[g * HALF : (g + 1) * HALF, :].T
    pack(out2)
    own2 = send_all(lambda p: out2.at[p], in2, 2)

    gain = 1.0 / math.sqrt(LINES * TILE * STEPS * TM / (2 * DEV * WIDTH))
    filler = jnp.zeros((HALF - SLOT, WIDTH), F32)
    contributions = []
    across = jnp.zeros((SLOT, WIDTH), F32)
    for s in range(2):
        sheet = (sums[s] * gain).astype(BF).astype(F32)
        tall = jnp.concatenate([sheet, filler], axis=0)
        adj_v[s] = jnp.concatenate([tall[:, :HALF].T, tall[:, HALF:].T], axis=0)

        def adjoint(i, state):
            totals, across = list(state[:NNZ]), state[NNZ]
            start = pl.multiple_of(i * CHUNK, CHUNK)
            weights = adj_v[s, pl.ds(start, CHUNK), :]
            for c in range(LANE_COMPS):
                weight = jnp.broadcast_to(weights[:, c : c + 1], (CHUNK, WIDTH))
                for k in range(NNZ):
                    block = kern_v[(s * NNZ + k) * COMPS + c, pl.ds(start, CHUNK), :].astype(F32) * weight
                    totals[k] = totals[k] + jnp.sum(block.reshape(CHUNK // 8, 8, WIDTH), axis=0)
            for c in range(LANE_COMPS, COMPS):
                left = jnp.where(wide_row == s * NNZ + i, sheet[c : c + 1], 0.0).astype(BF)
                across = across + nn(left, kern_v[(s * NNZ + i) * COMPS + c])
            return (*totals, across)

        state = lax.fori_loop(0, NNZ, adjoint, (*[jnp.zeros((8, WIDTH), F32)] * NNZ, across), unroll=2)
        contributions += [jnp.sum(total, axis=0, keepdims=True) for total in state[:NNZ]]
        across = state[NNZ]
    contributions = jnp.concatenate(contributions, axis=0) + across[:PAIRS]
    pieces = split(contributions, 2)
    stack = [piece[:, h * HALF : (h + 1) * HALF] for h in range(2) for piece in pieces]
    stack = jnp.concatenate(stack + [jnp.zeros((HALF - 4 * PAIRS, HALF), F32)], axis=0).astype(BF)
    stage_v[...] = nn(goal_v[...], stack)
    pack(out3)
    own3 = send_all(lambda p: out3.at[p], in3, 3)

    all_arrived(in2, 2, own2)
    unpack(in2)
    for s in range(2):
        for g in range(4):
            wide_v[pl.ds(g * HALF, HALF), pl.ds(s * HALF, HALF)] = (
                stage_v[pl.ds(s * 4 + g, DEV, stride=8), :].T.astype(BF)
            )
    rest = jnp.sum(nn(pick_v[...], wide_v[...]), axis=1, keepdims=True)

    def collect(l, _):
        lanes = pl.ds(pl.multiple_of(l * STEPS, STEPS), STEPS)
        every = nn(wide_v[...], hot_v[:, lanes])
        rank = rank_v[pl.ds(l, 1), :]
        value = jnp.zeros((SLOT, STEPS), F32)
        for r in range(CAP):
            value = value + jnp.where(rank == float(r), every[r * SLOT : (r + 1) * SLOT], 0.0)
        fold_v[pl.ds(pl.multiple_of(l * SLOT, SLOT), SLOT), :] = value
        return 0

    lax.fori_loop(0, LINES, collect, 0, unroll=2)
    onward = onward_v[...]
    late = nn(fold_v[:, WIDTH:].astype(BF), onward) + rest
    soon = nn(fold_v[:, :WIDTH].astype(BF), onward) + late[:, :1]
    scale = 1.0 / math.sqrt(STEPS * TM)
    saves = []
    for j, part in enumerate((soon[:, :HALF], soon[:, HALF:], late[:, :HALF], late[:, HALF:])):
        for l in range(LINES):
            off_v[pl.ds(j * DEV + l, SLOT, stride=LINES), :] = part[l * SLOT : (l + 1) * SLOT] * scale
        save = pltpu.make_async_copy(
            off_v.at[pl.ds(j * DEV, rows)], walk_hbm.at[:, pl.ds(j * HALF, HALF)], save_sem.at[j]
        )
        save.start()
        saves.append(save)

    all_arrived(in3, 3, own3)
    grad = jnp.sum(in3[...].astype(F32), axis=0)
    grad_ref[...] = jnp.concatenate([grad[:4], grad[4:]], axis=1)
    save = pltpu.make_async_copy(grad_ref, grad_hbm, save_sem.at[4])
    save.start()
    for save in saves + [save]:
        save.wait()
    for slot, dst in enumerate((mod_in, in1, in2, in3)):
        all_sent(dst, slot)


def deliver(grad_in, walk_in, grad_out, walk_out):
    walk_out[...] = walk_in[...]
    grad_out[...] = grad_in[...]


def shards(observed, increments, model, kernel, tile_index, station_of, line_length):
    rows = COMPS * LINES
    anywhere = pl.BlockSpec(memory_space=pl.ANY)
    message = pltpu.VMEM((DEV, 8, HALF), BF)
    grad_model, walk = pl.pallas_call(
        body,
        out_shape=(
            jax.ShapeDtypeStruct((4, WIDTH), F32),
            jax.ShapeDtypeStruct((rows, STEPS), F32),
        ),
        in_specs=[anywhere] * 7,
        out_specs=(anywhere, anywhere),
        scratch_shapes=[
            pltpu.VMEM((4, WIDTH), F32),
            pltpu.VMEM((rows, STEPS), F32),
            pltpu.VMEM((rows, STEPS), F32),
            pltpu.VMEM((4, WIDTH), F32),
            pltpu.SMEM((2, NNZ), I32),
            pltpu.VMEM((LINES, STEPS), I32),
            pltpu.SMEM((LINES,), I32),
            pltpu.VMEM((PAIRS * COMPS, WIDTH, WIDTH), BF),
            pltpu.VMEM((WIDTH, LINES * STEPS), BF),
            pltpu.VMEM((CAP * SLOT, LINES * STEPS), BF),
            pltpu.VMEM((LINES, STEPS), F32),
            pltpu.VMEM((4 * DEV, HALF), F32),
            pltpu.VMEM((DEV, CAP * SLOT), BF),
            pltpu.VMEM((CAP * SLOT, DEV), BF),
            pltpu.VMEM((DEV, DEV), BF),
            pltpu.VMEM((DEV, DEV), BF),
            pltpu.VMEM((DEV * 8, HALF), BF),
            pltpu.VMEM((WIDTH, WIDTH), BF),
            pltpu.VMEM((DEV * 8, HALF), F32),
            pltpu.VMEM((WIDTH, CAP * SLOT), F32),
            pltpu.VMEM((2, CAP * SLOT, HALF), F32),
            pltpu.VMEM((DEV, DEV), F32),
            pltpu.VMEM((SLOT, WIDTH), F32),
            pltpu.VMEM((2, SLOT, WIDTH), F32),
            pltpu.VMEM((2, WIDTH, HALF), F32),
            pltpu.VMEM((CAP * SLOT, WIDTH), BF),
            pltpu.VMEM((2, CAP * SLOT, HALF), F32),
            pltpu.VMEM((DEV, STEPS), F32),
            pltpu.VMEM((8, HALF), BF),
            message, message, message, message, message, message, message,
            pltpu.SemaphoreType.DMA((6,)),
            pltpu.SemaphoreType.DMA((5,)),
            pltpu.SemaphoreType.DMA,
            pltpu.SemaphoreType.DMA((4,)),
            pltpu.SemaphoreType.DMA((4,)),
            pltpu.SemaphoreType.DMA((4,)),
        ],
        compiler_params=pltpu.CompilerParams(
            collective_id=0, has_side_effects=True, vmem_limit_bytes=60 * 1024 * 1024
        ),
        name="invert",
    )(
        observed.reshape(rows, STEPS),
        increments.reshape(rows, STEPS),
        model,
        kernel.reshape(PAIRS * COMPS, WIDTH, WIDTH),
        tile_index,
        station_of,
        line_length,
    )
    grad_model, walk = pl.pallas_call(
        deliver,
        out_shape=(
            jax.ShapeDtypeStruct((4, WIDTH), F32),
            jax.ShapeDtypeStruct((rows, STEPS), F32),
        ),
        name="deliver",
    )(grad_model, walk)
    return grad_model, walk.reshape(COMPS, LINES, STEPS)


def solution(mesh):
    in_specs = (
        P(None, "tile", "tm"),
        P(None, "tile", "tm"),
        P(("tm", "tile"), None),
        P(("tm", "tile"), None, None, None, None),
        P(("tm", "tile"), None),
        P("tile", "tm"),
        P("tile"),
    )
    out_specs = (P(("tm", "tile"), None), P(None, "tile", "tm"))
    return jax.shard_map(shards, mesh=mesh, in_specs=in_specs, out_specs=out_specs, check_vma=False)
```

```python
import functools
import math

import jax
import jax.numpy as jnp
from jax import lax
from jax.experimental import pallas as pl
from jax.experimental.pallas import tpu as pltpu
from jax.sharding import PartitionSpec as P

MESH = pl.DeviceIdType.MESH
BF = jnp.bfloat16
F32 = jnp.float32
I32 = jnp.int32
TM = 16
TILE = 8
DEV = TM * TILE
CAP = 32
SLOT = 16
COMPS = 9
CHUNK = 64
LANE_COMPS = 6
LINES = 8
STEPS = 512
WIDTH = 256
HALF = 128
NNZ = 4
PAIRS = 8
LABEL = 9
LINE = 10
SPARE = 12
GRID = sorted(((x, y) for x in range(4) for y in range(4)), key=lambda o: -sum(min(v, 4 - v) for v in o))
COLUMNS = (4, 5, 3, 2, 6, 7, 1, 0)


def iota(shape, dim):
    return lax.broadcasted_iota(I32, shape, dim)


def nn(a, b):
    return lax.dot_general(a, b, (((1,), (0,)), ((), ())), preferred_element_type=F32)


def nt(a, b):
    return lax.dot_general(a, b, (((1,), (1,)), ((), ())), preferred_element_type=F32)


def split(x, count):
    pieces = []
    for _ in range(count):
        top = x.astype(BF).astype(F32)
        pieces.append(top)
        x = x - top
    return pieces


def ones(mask):
    return jnp.where(mask, 1.0, 0.0).astype(BF)


def spare_lane(line, comp):
    return (line * 4 + comp // 4) * SLOT + SPARE + comp % 4


def body(
    obs_hbm, inc_hbm, model_hbm, kern_ref, index_hbm, station_hbm, length_hbm,
    grad_hbm, walk_hbm,
    grad_ref, obs_ref, inc_ref, model_ref, index_ref, station_ref, length_ref,
    kern_v, hot_v, spread_v, rank_v, off_v, pick_v, put_v, before_v, after_v, goal_v, onward_v, stage_v, placed_v, table_v, early_v, cell_v, pred_v, adj_v, wide_v, res_v, fold_v,
    mod_out, mod_in, out1, in1, out2, in2, out3, in3,
    load_sem, save_sem, kern_sem, local_sem, send_sem, recv_sem,
):
    tm, tile = lax.axis_index("tm"), lax.axis_index("tile")
    me = tm * TILE + tile
    tiles = [lax.rem(tile + k, TILE) for k in COLUMNS]

    loads = [
        pltpu.make_async_copy(hbm, ref, load_sem.at[i])
        for i, (hbm, ref) in enumerate(
            (
                (inc_hbm, inc_ref), (obs_hbm, obs_ref), (model_hbm, model_ref),
                (station_hbm, station_ref), (length_hbm, length_ref), (index_hbm, index_ref),
            )
        )
    ]
    barrier = pltpu.get_barrier_semaphore()

    for dx, dy in GRID:
        row = lax.rem(tm // 4 + dx, 4) * 4 + lax.rem(lax.rem(tm, 4) + dy, 4)
        for k, t in zip(COLUMNS, tiles):
            if (dx, dy, k) != (0, 0, 0):
                pl.semaphore_signal(barrier, inc=1, device_id=(row, t), device_id_type=MESH)
    for load in loads:
        load.start()
    fetch = pltpu.make_async_copy(kern_ref, kern_v, kern_sem)
    fetch.start()

    def send_all(src_of, dst, slot):
        own = pltpu.make_async_copy(src_of(me), dst.at[me], local_sem.at[slot])
        own.start()
        for dx, dy in GRID:
            row = lax.rem(tm // 4 + dx, 4) * 4 + lax.rem(lax.rem(tm, 4) + dy, 4)
            for k, t in zip(COLUMNS, tiles):
                if (dx, dy, k) != (0, 0, 0):
                    pltpu.make_async_remote_copy(
                        src_ref=src_of(row * TILE + t), dst_ref=dst.at[me],
                        send_sem=send_sem.at[slot], recv_sem=recv_sem.at[slot],
                        device_id=(row, t), device_id_type=MESH,
                    ).start()
        return own

    def all_arrived(dst, slot, own):
        own.wait()
        span = dst.at[pl.ds(0, DEV - 1)]
        pltpu.make_async_copy(span, span, recv_sem.at[slot]).wait()

    def all_sent(dst, slot):
        span = dst.at[pl.ds(0, DEV - 1)]
        pltpu.make_async_copy(span, span, send_sem.at[slot]).wait()

    for load in loads:
        load.wait()
    cells = model_ref[...]
    mod_out[...] = jnp.concatenate([cells[:, :HALF], cells[:, HALF:]], axis=0).astype(BF)

    upto = ones(iota((WIDTH, WIDTH), 0) <= iota((WIDTH, WIDTH), 1))
    steps = inc_ref[...]
    rows = COMPS * LINES
    first = jnp.concatenate(split(steps[:, :WIDTH], 3), axis=0).astype(BF)
    second = jnp.concatenate(split(steps[:, WIDTH:], 3), axis=0).astype(BF)
    first, second = nn(first, upto), nn(second, upto)
    first = first[:rows] + first[rows : 2 * rows] + first[2 * rows :]
    second = second[:rows] + second[rows : 2 * rows] + second[2 * rows :]
    second = second + first[:, WIDTH - 1 :]
    totals = second[:, WIDTH - 1 :]
    first = first - obs_ref[:, :WIDTH]
    second = second - obs_ref[:, WIDTH:]
    for j, part in enumerate((first[:, :HALF], first[:, HALF:], second[:, :HALF], second[:, HALF:])):
        off_v[pl.ds(j * DEV, rows), :] = part
        off_v[pl.ds(j * DEV + rows, DEV - rows), :] = jnp.zeros((DEV - rows, HALF), F32)

    def one_line(l, base):
        lanes = pl.ds(l * STEPS, STEPS)
        station = station_ref[pl.ds(l, 1), :]
        owner = station // WIDTH
        inner = station % WIDTH
        line_place = (owner % 2) * HALF + owner // 2
        hit = iota((WIDTH, STEPS), 0) == line_place
        hot = ones(hit)
        hot_v[:, lanes] = hot
        ranks = []
        for h in range(2):
            part = slice(h * WIDTH, (h + 1) * WIDTH)
            count = nn(hot[:, part], upto)
            ranks.append(jnp.sum(jnp.where(hit[:, part], count + base, 0.0), axis=0, keepdims=True))
            base = base + count[:, WIDTH - 1 :]
        rank = jnp.concatenate(ranks, axis=1) - 1.0
        rank_v[pl.ds(l, 1), :] = rank
        position = tm * STEPS + iota((1, STEPS), 1)
        label = jnp.where(position < length_ref[l], inner + 1, 0).astype(F32)
        comp = iota((SLOT, STEPS), 0)
        values = jnp.concatenate([off_v[pl.ds(j * DEV + l, SLOT, stride=LINES), :] for j in range(4)], axis=1)
        values = jnp.where(comp == LABEL, label, values)
        values = jnp.where(comp == LINE, float(l), values)
        for r in range(CAP):
            spread_v[pl.ds(r * SLOT, SLOT), lanes] = jnp.where(rank == float(r), values, 0.0).astype(BF)
        return base

    def place(l):
        lanes = pl.ds(l * STEPS, STEPS)
        fresh = nt(hot_v[:, lanes], spread_v[:, lanes])
        placed_v[...] = fresh if l == 0 else placed_v[...] + fresh

    base = jnp.zeros((WIDTH, 1), F32)
    for l in range(LINES):
        base = one_line(l, base)
        if l:
            place(l - 1)
        if l == 5:
            pl.semaphore_wait(barrier, DEV - 1)
            own_mod = send_all(lambda p: mod_out, mod_in, 0)
    place(LINES - 1)
    row = iota((rows, CAP * SLOT), 0)
    at_spare = iota((rows, CAP * SLOT), 1) == spare_lane(row % LINES, row // LINES)
    for s, part in enumerate(split(totals, 2)):
        extra = jnp.sum(jnp.where(at_spare, part, 0.0), axis=0, keepdims=True)
        half = placed_v[pl.ds(s * HALF, HALF), :] + extra
        for g in range(4):
            stage_v[pl.ds(s * 4 + g, DEV, stride=8), :] = half[:, g * HALF : (g + 1) * HALF]

    def pack(dst):
        dst[...] = stage_v[...].reshape(DEV, 8, HALF).astype(BF)

    def unpack(src):
        stage_v[...] = src[...].astype(F32).reshape(DEV * 8, HALF)

    pack(out1)
    own1 = send_all(lambda p: out1.at[p], in1, 1)

    q_row = iota((DEV, CAP * SLOT), 0)
    pick_v[...] = ones(
        (iota((DEV, CAP * SLOT), 1) == spare_lane(q_row // SLOT, q_row % SLOT)) & (q_row % SLOT < COMPS)
    )
    q_lane = iota((CAP * SLOT, DEV), 1)
    put_v[...] = ones(
        (iota((CAP * SLOT, DEV), 0) == spare_lane(q_lane // SLOT, q_lane % SLOT)) & (q_lane % SLOT < COMPS)
    )
    source, target = iota((DEV, DEV), 0), iota((DEV, DEV), 1)
    same_lines = source % TILE == target % TILE
    before_v[...] = ones(same_lines & (source // TILE < target // TILE))
    after_v[...] = ones(same_lines & (source // TILE > target // TILE))
    lane = iota((1, HALF), 1)
    goal = jnp.full((1, HALF), -8, I32)
    for q in range(PAIRS):
        cell = index_ref[q // NNZ, q % NNZ]
        goal = jnp.where(lane % PAIRS == q, (cell // 4) * 8 + cell % 4, goal)
    goal = jnp.where(lane < 4 * PAIRS, goal + 4 * (lane // (2 * PAIRS)), -8)
    goal_v[...] = ones(iota((DEV * 8, HALF), 0) == goal)
    onward_v[...] = ones(iota((WIDTH, WIDTH), 0) >= iota((WIDTH, WIDTH), 1))
    fetch.wait()
    all_arrived(mod_in, 0, own_mod)
    pair_row = iota((SLOT, DEV * 8), 0)
    pair_lane = iota((SLOT, DEV * 8), 1)
    base_row = jnp.full((SLOT, DEV * 8), -8, I32)
    for q in range(PAIRS):
        cell = index_ref[q // NNZ, q % NNZ]
        base_row = jnp.where(pair_row == q, (cell // 4) * 8 + cell % 4, base_row)
    every = mod_in[...].reshape(DEV * 8, HALF)
    chosen = jnp.concatenate([nn(ones(pair_lane == base_row + 4 * h), every) for h in range(2)], axis=1)
    cell_v[...] = chosen
    comp_row = iota((SLOT, HALF), 0)
    wide_row = iota((SLOT, WIDTH), 0)
    for s in range(2):
        vectors = [cell_v[pl.ds(s * NNZ + k, 1), :] for k in range(NNZ)]

        def forward(i, state):
            halves, across = list(state[:2]), state[2]
            last = LANE_COMPS + i
            for c in (2 * i, 2 * i + 1):
                sums = []
                for j in range(0, WIDTH, CHUNK):
                    total = jnp.zeros((CHUNK, HALF), F32)
                    for k in range(NNZ):
                        block = kern_v[(s * NNZ + k) * COMPS + c, pl.ds(j, CHUNK), :].astype(F32) * vectors[k]
                        total = total + block[:, :HALF] + block[:, HALF:]
                    sums.append(total)
                for h in range(2):
                    tall = jnp.concatenate(sums[h * HALF // CHUNK : (h + 1) * HALF // CHUNK], axis=0).T
                    halves[h] = jnp.where(comp_row == c, jnp.sum(tall, axis=0, keepdims=True), halves[h])
            for k in range(NNZ):
                left = jnp.where(wide_row == last, vectors[k], 0.0).astype(BF)
                across = across + nt(left, kern_v[(s * NNZ + k) * COMPS + last])
            return (*halves, across)

        state = lax.fori_loop(
            0, LANE_COMPS // 2, forward, unroll=3, init_val=(*[jnp.zeros((SLOT, HALF), F32)] * 2, jnp.zeros((SLOT, WIDTH), F32))
        )
        for h in range(2):
            part = slice(h * HALF, (h + 1) * HALF)
            pred_v[s, :, pl.ds(h * HALF, HALF)] = state[h] + state[2][:, part]

    all_arrived(in1, 1, own1)
    unpack(in1)
    for s in range(2):
        for g in range(4):
            table_v[s, pl.ds(g * HALF, HALF), :] = stage_v[pl.ds(s * 4 + g, DEV, stride=8), :].T
    early = jnp.zeros((DEV, DEV), F32)
    for s in range(2):
        part = nn(pick_v[...], table_v[s].astype(BF))
        early = early + nn(part.astype(BF), before_v[...])
    early_v[...] = early

    lane_count = 2 * HALF
    slot_row = iota((SLOT, lane_count), 0)
    station_row = iota((WIDTH, lane_count), 0)
    tables = [[pred_v[s, :, pl.ds(h * HALF, HALF)] for h in range(2)] for s in range(2)]

    def slots(i, carry):
        totals = list(carry[:2])
        lines = list(carry[2:])
        start = pl.multiple_of(i * 2 * SLOT, 2 * SLOT)
        for s in range(2):
            pair = [table_v[s, pl.ds(start + j * SLOT, SLOT), :] for j in range(2)]
            got = jnp.concatenate(pair, axis=1)
            label = got[LABEL : LABEL + 1]
            line = got[LINE : LINE + 1]
            match = ones(station_row == label.astype(I32) - 1)
            picked = []
            for part in pair:
                at = jnp.broadcast_to(jnp.maximum(part[LABEL : LABEL + 1].astype(I32) - 1, 0), (SLOT, HALF))
                lane = at % HALF
                low = jnp.take_along_axis(tables[s][0], lane, axis=1)
                high = jnp.take_along_axis(tables[s][1], lane, axis=1)
                picked.append(jnp.where(at >= HALF, high, low))
            value = jnp.concatenate(picked, axis=1) + got
            for l in range(LINES):
                walk = early_v[pl.ds(l * SLOT, SLOT), :]
                value = value + jnp.where(line == float(l), jnp.concatenate([walk, walk], axis=1), 0.0)
            value = jnp.where((label > 0.0) & (slot_row < COMPS), value, 0.0)
            res_v[s, pl.ds(start, SLOT), :] = value[:, :HALF]
            res_v[s, pl.ds(start + SLOT, SLOT), :] = value[:, HALF:]
            for l in range(LINES):
                mine = jnp.where(line == float(l), value, 0.0)
                lines[l] = lines[l] + mine[:, :HALF] + mine[:, HALF:]
            totals[s] = totals[s] + nt(jnp.concatenate(split(value, 3), axis=0).astype(BF), match)
        return (*totals, *lines)

    carry = lax.fori_loop(
        0, CAP // 2, slots, unroll=4, init_val=
        (*[jnp.zeros((3 * SLOT, WIDTH), F32)] * 2, *[jnp.zeros((SLOT, HALF), F32)] * LINES),
    )
    sums = [total[:SLOT] + total[SLOT : 2 * SLOT] + total[2 * SLOT :] for total in carry[:2]]
    line_sums = list(carry[2:])

    gathered = jnp.concatenate(line_sums, axis=0)
    three = nn(jnp.concatenate(split(gathered, 3), axis=0).astype(BF), after_v[...])
    beyond = three[:DEV] + three[DEV : 2 * DEV] + three[2 * DEV :]
    for s, part in enumerate(split(beyond, 2)):
        full = res_v[s] + nn(put_v[...], part.astype(BF))
        for g in range(4):
            stage_v[pl.ds(s * 4 + g, DEV, stride=8), :] = full[g * HALF : (g + 1) * HALF, :].T
    pack(out2)
    own2 = send_all(lambda p: out2.at[p], in2, 2)

    gain = 1.0 / math.sqrt(LINES * TILE * STEPS * TM / (2 * DEV * WIDTH))
    filler = jnp.zeros((HALF - SLOT, WIDTH), F32)
    contributions = []
    across = jnp.zeros((SLOT, WIDTH), F32)
    for s in range(2):
        sheet = (sums[s] * gain).astype(BF).astype(F32)
        tall = jnp.concatenate([sheet, filler], axis=0)
        adj_v[s] = jnp.concatenate([tall[:, :HALF].T, tall[:, HALF:].T], axis=0)

        def adjoint(i, state):
            totals, across = list(state[:NNZ]), state[NNZ]
            start = pl.multiple_of(i * CHUNK, CHUNK)
            weights = adj_v[s, pl.ds(start, CHUNK), :]
            for c in range(LANE_COMPS):
                weight = jnp.broadcast_to(weights[:, c : c + 1], (CHUNK, WIDTH))
                for k in range(NNZ):
                    block = kern_v[(s * NNZ + k) * COMPS + c, pl.ds(start, CHUNK), :].astype(F32) * weight
                    totals[k] = totals[k] + jnp.sum(block.reshape(CHUNK // 8, 8, WIDTH), axis=0)
            for c in range(LANE_COMPS, COMPS):
                left = jnp.where(wide_row == s * NNZ + i, sheet[c : c + 1], 0.0).astype(BF)
                across = across + nn(left, kern_v[(s * NNZ + i) * COMPS + c])
            return (*totals, across)

        state = lax.fori_loop(0, NNZ, adjoint, (*[jnp.zeros((8, WIDTH), F32)] * NNZ, across), unroll=2)
        contributions += [jnp.sum(total, axis=0, keepdims=True) for total in state[:NNZ]]
        across = state[NNZ]
    contributions = jnp.concatenate(contributions, axis=0) + across[:PAIRS]
    pieces = split(contributions, 2)
    stack = [piece[:, h * HALF : (h + 1) * HALF] for h in range(2) for piece in pieces]
    stack = jnp.concatenate(stack + [jnp.zeros((HALF - 4 * PAIRS, HALF), F32)], axis=0).astype(BF)
    stage_v[...] = nn(goal_v[...], stack)
    pack(out3)
    own3 = send_all(lambda p: out3.at[p], in3, 3)

    all_arrived(in2, 2, own2)
    unpack(in2)
    for s in range(2):
        for g in range(4):
            wide_v[pl.ds(g * HALF, HALF), pl.ds(s * HALF, HALF)] = (
                stage_v[pl.ds(s * 4 + g, DEV, stride=8), :].T.astype(BF)
            )
    rest = jnp.sum(nn(pick_v[...], wide_v[...]), axis=1, keepdims=True)

    def collect(l, _):
        lanes = pl.ds(pl.multiple_of(l * STEPS, STEPS), STEPS)
        every = nn(wide_v[...], hot_v[:, lanes])
        rank = rank_v[pl.ds(l, 1), :]
        value = jnp.zeros((SLOT, STEPS), F32)
        for r in range(CAP):
            value = value + jnp.where(rank == float(r), every[r * SLOT : (r + 1) * SLOT], 0.0)
        fold_v[pl.ds(pl.multiple_of(l * SLOT, SLOT), SLOT), :] = value
        return 0

    lax.fori_loop(0, LINES, collect, 0, unroll=4)
    onward = onward_v[...]
    late = nn(fold_v[:, WIDTH:].astype(BF), onward) + rest
    soon = nn(fold_v[:, :WIDTH].astype(BF), onward) + late[:, :1]
    scale = 1.0 / math.sqrt(STEPS * TM)
    saves = []
    for j, part in enumerate((soon[:, :HALF], soon[:, HALF:], late[:, :HALF], late[:, HALF:])):
        for l in range(LINES):
            off_v[pl.ds(j * DEV + l, SLOT, stride=LINES), :] = part[l * SLOT : (l + 1) * SLOT] * scale
        save = pltpu.make_async_copy(
            off_v.at[pl.ds(j * DEV, rows)], walk_hbm.at[:, pl.ds(j * HALF, HALF)], save_sem.at[j]
        )
        save.start()
        saves.append(save)

    all_arrived(in3, 3, own3)
    grad = jnp.sum(in3[...].astype(F32), axis=0)
    grad_ref[...] = jnp.concatenate([grad[:4], grad[4:]], axis=1)
    save = pltpu.make_async_copy(grad_ref, grad_hbm, save_sem.at[4])
    save.start()
    for save in saves + [save]:
        save.wait()
    for slot, dst in enumerate((mod_in, in1, in2, in3)):
        all_sent(dst, slot)


def deliver(grad_in, walk_in, grad_out, walk_out):
    walk_out[...] = walk_in[...]
    grad_out[...] = grad_in[...]


def shards(observed, increments, model, kernel, tile_index, station_of, line_length):
    rows = COMPS * LINES
    anywhere = pl.BlockSpec(memory_space=pl.ANY)
    message = pltpu.VMEM((DEV, 8, HALF), BF)
    grad_model, walk = pl.pallas_call(
        body,
        out_shape=(
            jax.ShapeDtypeStruct((4, WIDTH), F32),
            jax.ShapeDtypeStruct((rows, STEPS), F32),
        ),
        in_specs=[anywhere] * 7,
        out_specs=(anywhere, anywhere),
        scratch_shapes=[
            pltpu.VMEM((4, WIDTH), F32),
            pltpu.VMEM((rows, STEPS), F32),
            pltpu.VMEM((rows, STEPS), F32),
            pltpu.VMEM((4, WIDTH), F32),
            pltpu.SMEM((2, NNZ), I32),
            pltpu.VMEM((LINES, STEPS), I32),
            pltpu.SMEM((LINES,), I32),
            pltpu.VMEM((PAIRS * COMPS, WIDTH, WIDTH), BF),
            pltpu.VMEM((WIDTH, LINES * STEPS), BF),
            pltpu.VMEM((CAP * SLOT, LINES * STEPS), BF),
            pltpu.VMEM((LINES, STEPS), F32),
            pltpu.VMEM((4 * DEV, HALF), F32),
            pltpu.VMEM((DEV, CAP * SLOT), BF),
            pltpu.VMEM((CAP * SLOT, DEV), BF),
            pltpu.VMEM((DEV, DEV), BF),
            pltpu.VMEM((DEV, DEV), BF),
            pltpu.VMEM((DEV * 8, HALF), BF),
            pltpu.VMEM((WIDTH, WIDTH), BF),
            pltpu.VMEM((DEV * 8, HALF), F32),
            pltpu.VMEM((WIDTH, CAP * SLOT), F32),
            pltpu.VMEM((2, CAP * SLOT, HALF), F32),
            pltpu.VMEM((DEV, DEV), F32),
            pltpu.VMEM((SLOT, WIDTH), F32),
            pltpu.VMEM((2, SLOT, WIDTH), F32),
            pltpu.VMEM((2, WIDTH, HALF), F32),
            pltpu.VMEM((CAP * SLOT, WIDTH), BF),
            pltpu.VMEM((2, CAP * SLOT, HALF), F32),
            pltpu.VMEM((DEV, STEPS), F32),
            pltpu.VMEM((8, HALF), BF),
            message, message, message, message, message, message, message,
            pltpu.SemaphoreType.DMA((6,)),
            pltpu.SemaphoreType.DMA((5,)),
            pltpu.SemaphoreType.DMA,
            pltpu.SemaphoreType.DMA((4,)),
            pltpu.SemaphoreType.DMA((4,)),
            pltpu.SemaphoreType.DMA((4,)),
        ],
        compiler_params=pltpu.CompilerParams(
            collective_id=0, has_side_effects=True, vmem_limit_bytes=60 * 1024 * 1024
        ),
        name="invert",
    )(
        observed.reshape(rows, STEPS),
        increments.reshape(rows, STEPS),
        model,
        kernel.reshape(PAIRS * COMPS, WIDTH, WIDTH),
        tile_index,
        station_of,
        line_length,
    )
    grad_model, walk = pl.pallas_call(
        deliver,
        out_shape=(
            jax.ShapeDtypeStruct((4, WIDTH), F32),
            jax.ShapeDtypeStruct((rows, STEPS), F32),
        ),
        name="deliver",
    )(grad_model, walk)
    return grad_model, walk.reshape(COMPS, LINES, STEPS)


def solution(mesh):
    in_specs = (
        P(None, "tile", "tm"),
        P(None, "tile", "tm"),
        P(("tm", "tile"), None),
        P(("tm", "tile"), None, None, None, None),
        P(("tm", "tile"), None),
        P("tile", "tm"),
        P("tile"),
    )
    out_specs = (P(("tm", "tile"), None), P(None, "tile", "tm"))
    return jax.shard_map(shards, mesh=mesh, in_specs=in_specs, out_specs=out_specs, check_vma=False)
```

```python
import functools
import math

import jax
import jax.numpy as jnp
from jax import lax
from jax.experimental import pallas as pl
from jax.experimental.pallas import tpu as pltpu
from jax.sharding import PartitionSpec as P

MESH = pl.DeviceIdType.MESH
BF = jnp.bfloat16
F32 = jnp.float32
I32 = jnp.int32
TM = 16
TILE = 8
DEV = TM * TILE
CAP = 32
SLOT = 16
COMPS = 9
CHUNK = 64
LANE_COMPS = 6
LINES = 8
STEPS = 512
WIDTH = 256
HALF = 128
NNZ = 4
PAIRS = 8
LABEL = 9
LINE = 10
SPARE = 12
GRID = sorted(((x, y) for x in range(4) for y in range(4)), key=lambda o: -sum(min(v, 4 - v) for v in o))
COLUMNS = (4, 5, 3, 2, 6, 7, 1, 0)


def iota(shape, dim):
    return lax.broadcasted_iota(I32, shape, dim)


def nn(a, b):
    return lax.dot_general(a, b, (((1,), (0,)), ((), ())), preferred_element_type=F32)


def nt(a, b):
    return lax.dot_general(a, b, (((1,), (1,)), ((), ())), preferred_element_type=F32)


def split(x, count):
    pieces = []
    for _ in range(count):
        top = x.astype(BF).astype(F32)
        pieces.append(top)
        x = x - top
    return pieces


def ones(mask):
    return jnp.where(mask, 1.0, 0.0).astype(BF)


def spare_lane(line, comp):
    return (line * 4 + comp // 4) * SLOT + SPARE + comp % 4


def body(
    obs_hbm, inc_hbm, model_hbm, kern_ref, index_hbm, station_hbm, length_hbm,
    grad_hbm, walk_hbm,
    grad_ref, obs_ref, inc_ref, model_ref, index_ref, station_ref, length_ref,
    kern_v, hot_v, spread_v, rank_v, off_v, pick_v, put_v, before_v, after_v, goal_v, onward_v, stage_v, placed_v, table_v, early_v, cell_v, pred_v, adj_v, wide_v, res_v, fold_v,
    mod_out, mod_in, out1, in1, out2, in2, out3, in3,
    load_sem, save_sem, kern_sem, local_sem, send_sem, recv_sem,
):
    tm, tile = lax.axis_index("tm"), lax.axis_index("tile")
    me = tm * TILE + tile
    tiles = [lax.rem(tile + k, TILE) for k in COLUMNS]

    loads = [
        pltpu.make_async_copy(hbm, ref, load_sem.at[i])
        for i, (hbm, ref) in enumerate(
            (
                (inc_hbm, inc_ref), (obs_hbm, obs_ref), (model_hbm, model_ref),
                (station_hbm, station_ref), (length_hbm, length_ref), (index_hbm, index_ref),
            )
        )
    ]
    barrier = pltpu.get_barrier_semaphore()

    for dx, dy in GRID:
        row = lax.rem(tm // 4 + dx, 4) * 4 + lax.rem(lax.rem(tm, 4) + dy, 4)
        for k, t in zip(COLUMNS, tiles):
            if (dx, dy, k) != (0, 0, 0):
                pl.semaphore_signal(barrier, inc=1, device_id=(row, t), device_id_type=MESH)
    for load in loads:
        load.start()
    fetch = pltpu.make_async_copy(kern_ref, kern_v, kern_sem)

    rows_of = {
        (dx, dy): lax.rem(tm // 4 + dx, 4) * 4 + lax.rem(lax.rem(tm, 4) + dy, 4) for dx, dy in GRID
    }

    def send_all(src_of, dst, slot):
        own = pltpu.make_async_copy(src_of(me), dst.at[me], local_sem.at[slot])
        own.start()
        for j in range(DEV):
            (dx, dy), (k, t) = GRID[(5 * j + j // TM) % TM], (COLUMNS[j // TM], tiles[j // TM])
            row = rows_of[dx, dy]
            if (dx, dy, k) != (0, 0, 0):
                pltpu.make_async_remote_copy(
                    src_ref=src_of(row * TILE + t), dst_ref=dst.at[me],
                    send_sem=send_sem.at[slot], recv_sem=recv_sem.at[slot],
                    device_id=(row, t), device_id_type=MESH,
                ).start()
        return own

    def all_arrived(dst, slot, own):
        own.wait()
        span = dst.at[pl.ds(0, DEV - 1)]
        pltpu.make_async_copy(span, span, recv_sem.at[slot]).wait()

    def all_sent(dst, slot):
        span = dst.at[pl.ds(0, DEV - 1)]
        pltpu.make_async_copy(span, span, send_sem.at[slot]).wait()

    for load in loads:
        load.wait()
    fetch.start()
    cells = model_ref[...]
    mod_out[...] = jnp.concatenate([cells[:, :HALF], cells[:, HALF:]], axis=0).astype(BF)

    upto = ones(iota((WIDTH, WIDTH), 0) <= iota((WIDTH, WIDTH), 1))
    steps = inc_ref[...]
    rows = COMPS * LINES
    first = jnp.concatenate(split(steps[:, :WIDTH], 3), axis=0).astype(BF)
    second = jnp.concatenate(split(steps[:, WIDTH:], 3), axis=0).astype(BF)
    first, second = nn(first, upto), nn(second, upto)
    first = first[:rows] + first[rows : 2 * rows] + first[2 * rows :]
    second = second[:rows] + second[rows : 2 * rows] + second[2 * rows :]
    second = second + first[:, WIDTH - 1 :]
    totals = second[:, WIDTH - 1 :]
    first = first - obs_ref[:, :WIDTH]
    second = second - obs_ref[:, WIDTH:]
    for j, part in enumerate((first[:, :HALF], first[:, HALF:], second[:, :HALF], second[:, HALF:])):
        off_v[pl.ds(j * DEV, rows), :] = part
        off_v[pl.ds(j * DEV + rows, DEV - rows), :] = jnp.zeros((DEV - rows, HALF), F32)

    def one_line(l, base):
        lanes = pl.ds(l * STEPS, STEPS)
        station = station_ref[pl.ds(l, 1), :]
        owner = station // WIDTH
        inner = station % WIDTH
        line_place = (owner % 2) * HALF + owner // 2
        hit = iota((WIDTH, STEPS), 0) == line_place
        hot = ones(hit)
        hot_v[:, lanes] = hot
        ranks = []
        for h in range(2):
            part = slice(h * WIDTH, (h + 1) * WIDTH)
            count = nn(hot[:, part], upto)
            ranks.append(jnp.sum(jnp.where(hit[:, part], count + base, 0.0), axis=0, keepdims=True))
            base = base + count[:, WIDTH - 1 :]
        rank = jnp.concatenate(ranks, axis=1) - 1.0
        rank_v[pl.ds(l, 1), :] = rank
        position = tm * STEPS + iota((1, STEPS), 1)
        label = jnp.where(position < length_ref[l], inner + 1, 0).astype(F32)
        comp = iota((SLOT, STEPS), 0)
        values = jnp.concatenate([off_v[pl.ds(j * DEV + l, SLOT, stride=LINES), :] for j in range(4)], axis=1)
        values = jnp.where(comp == LABEL, label, values)
        values = jnp.where(comp == LINE, float(l), values)
        for r in range(CAP):
            spread_v[pl.ds(r * SLOT, SLOT), lanes] = jnp.where(rank == float(r), values, 0.0).astype(BF)
        return base

    def place(l):
        lanes = pl.ds(l * STEPS, STEPS)
        fresh = nt(hot_v[:, lanes], spread_v[:, lanes])
        placed_v[...] = fresh if l == 0 else placed_v[...] + fresh

    base = jnp.zeros((WIDTH, 1), F32)
    for l in range(LINES):
        base = one_line(l, base)
        if l:
            place(l - 1)
        if l == 5:
            pl.semaphore_wait(barrier, DEV - 1)
            own_mod = send_all(lambda p: mod_out, mod_in, 0)
    place(LINES - 1)
    row = iota((rows, CAP * SLOT), 0)
    at_spare = iota((rows, CAP * SLOT), 1) == spare_lane(row % LINES, row // LINES)
    for s, part in enumerate(split(totals, 2)):
        extra = jnp.sum(jnp.where(at_spare, part, 0.0), axis=0, keepdims=True)
        half = placed_v[pl.ds(s * HALF, HALF), :] + extra
        for g in range(4):
            stage_v[pl.ds(s * 4 + g, DEV, stride=8), :] = half[:, g * HALF : (g + 1) * HALF]

    def pack(dst):
        dst[...] = stage_v[...].reshape(DEV, 8, HALF).astype(BF)

    def unpack(src):
        stage_v[...] = src[...].astype(F32).reshape(DEV * 8, HALF)

    pack(out1)
    own1 = send_all(lambda p: out1.at[p], in1, 1)

    q_row = iota((DEV, CAP * SLOT), 0)
    pick_v[...] = ones(
        (iota((DEV, CAP * SLOT), 1) == spare_lane(q_row // SLOT, q_row % SLOT)) & (q_row % SLOT < COMPS)
    )
    q_lane = iota((CAP * SLOT, DEV), 1)
    put_v[...] = ones(
        (iota((CAP * SLOT, DEV), 0) == spare_lane(q_lane // SLOT, q_lane % SLOT)) & (q_lane % SLOT < COMPS)
    )
    source, target = iota((DEV, DEV), 0), iota((DEV, DEV), 1)
    same_lines = source % TILE == target % TILE
    before_v[...] = ones(same_lines & (source // TILE < target // TILE))
    after_v[...] = ones(same_lines & (source // TILE > target // TILE))
    lane = iota((1, HALF), 1)
    goal = jnp.full((1, HALF), -8, I32)
    for q in range(PAIRS):
        cell = index_ref[q // NNZ, q % NNZ]
        goal = jnp.where(lane % PAIRS == q, (cell // 4) * 8 + cell % 4, goal)
    goal = jnp.where(lane < 4 * PAIRS, goal + 4 * (lane // (2 * PAIRS)), -8)
    goal_v[...] = ones(iota((DEV * 8, HALF), 0) == goal)
    onward_v[...] = ones(iota((WIDTH, WIDTH), 0) >= iota((WIDTH, WIDTH), 1))
    fetch.wait()
    all_arrived(mod_in, 0, own_mod)
    pair_row = iota((SLOT, DEV * 8), 0)
    pair_lane = iota((SLOT, DEV * 8), 1)
    base_row = jnp.full((SLOT, DEV * 8), -8, I32)
    for q in range(PAIRS):
        cell = index_ref[q // NNZ, q % NNZ]
        base_row = jnp.where(pair_row == q, (cell // 4) * 8 + cell % 4, base_row)
    every = mod_in[...].reshape(DEV * 8, HALF)
    chosen = jnp.concatenate([nn(ones(pair_lane == base_row + 4 * h), every) for h in range(2)], axis=1)
    cell_v[...] = chosen
    comp_row = iota((SLOT, HALF), 0)
    wide_row = iota((SLOT, WIDTH), 0)
    for s in range(2):
        vectors = [cell_v[pl.ds(s * NNZ + k, 1), :] for k in range(NNZ)]

        def forward(i, state):
            halves, across = list(state[:2]), state[2]
            last = LANE_COMPS + i
            for c in (2 * i, 2 * i + 1):
                sums = []
                for j in range(0, WIDTH, CHUNK):
                    total = jnp.zeros((CHUNK, HALF), F32)
                    for k in range(NNZ):
                        block = kern_v[(s * NNZ + k) * COMPS + c, pl.ds(j, CHUNK), :].astype(F32) * vectors[k]
                        total = total + block[:, :HALF] + block[:, HALF:]
                    sums.append(total)
                for h in range(2):
                    tall = jnp.concatenate(sums[h * HALF // CHUNK : (h + 1) * HALF // CHUNK], axis=0).T
                    halves[h] = jnp.where(comp_row == c, jnp.sum(tall, axis=0, keepdims=True), halves[h])
            for k in range(NNZ):
                left = jnp.where(wide_row == last, vectors[k], 0.0).astype(BF)
                across = across + nt(left, kern_v[(s * NNZ + k) * COMPS + last])
            return (*halves, across)

        state = lax.fori_loop(
            0, LANE_COMPS // 2, forward, unroll=3, init_val=(*[jnp.zeros((SLOT, HALF), F32)] * 2, jnp.zeros((SLOT, WIDTH), F32))
        )
        for h in range(2):
            part = slice(h * HALF, (h + 1) * HALF)
            pred_v[s, :, pl.ds(h * HALF, HALF)] = state[h] + state[2][:, part]

    all_arrived(in1, 1, own1)
    unpack(in1)
    for s in range(2):
        for g in range(4):
            table_v[s, pl.ds(g * HALF, HALF), :] = stage_v[pl.ds(s * 4 + g, DEV, stride=8), :].T
    early = jnp.zeros((DEV, DEV), F32)
    for s in range(2):
        part = nn(pick_v[...], table_v[s].astype(BF))
        early = early + nn(part.astype(BF), before_v[...])
    early_v[...] = early

    lane_count = 2 * HALF
    slot_row = iota((SLOT, lane_count), 0)
    station_row = iota((WIDTH, lane_count), 0)
    tables = [[pred_v[s, :, pl.ds(h * HALF, HALF)] for h in range(2)] for s in range(2)]

    def slots(i, carry):
        totals = list(carry[:2])
        lines = list(carry[2:])
        start = pl.multiple_of(i * 2 * SLOT, 2 * SLOT)
        for s in range(2):
            pair = [table_v[s, pl.ds(start + j * SLOT, SLOT), :] for j in range(2)]
            got = jnp.concatenate(pair, axis=1)
            label = got[LABEL : LABEL + 1]
            line = got[LINE : LINE + 1]
            match = ones(station_row == label.astype(I32) - 1)
            picked = []
            for part in pair:
                at = jnp.broadcast_to(jnp.maximum(part[LABEL : LABEL + 1].astype(I32) - 1, 0), (SLOT, HALF))
                lane = at % HALF
                low = jnp.take_along_axis(tables[s][0], lane, axis=1)
                high = jnp.take_along_axis(tables[s][1], lane, axis=1)
                picked.append(jnp.where(at >= HALF, high, low))
            value = jnp.concatenate(picked, axis=1) + got
            for l in range(LINES):
                walk = early_v[pl.ds(l * SLOT, SLOT), :]
                value = value + jnp.where(line == float(l), jnp.concatenate([walk, walk], axis=1), 0.0)
            value = jnp.where((label > 0.0) & (slot_row < COMPS), value, 0.0)
            res_v[s, pl.ds(start, SLOT), :] = value[:, :HALF]
            res_v[s, pl.ds(start + SLOT, SLOT), :] = value[:, HALF:]
            for l in range(LINES):
                mine = jnp.where(line == float(l), value, 0.0)
                lines[l] = lines[l] + mine[:, :HALF] + mine[:, HALF:]
            totals[s] = totals[s] + nt(jnp.concatenate(split(value, 3), axis=0).astype(BF), match)
        return (*totals, *lines)

    carry = lax.fori_loop(
        0, CAP // 2, slots, unroll=4, init_val=
        (*[jnp.zeros((3 * SLOT, WIDTH), F32)] * 2, *[jnp.zeros((SLOT, HALF), F32)] * LINES),
    )
    sums = [total[:SLOT] + total[SLOT : 2 * SLOT] + total[2 * SLOT :] for total in carry[:2]]
    line_sums = list(carry[2:])

    gathered = jnp.concatenate(line_sums, axis=0)
    three = nn(jnp.concatenate(split(gathered, 3), axis=0).astype(BF), after_v[...])
    beyond = three[:DEV] + three[DEV : 2 * DEV] + three[2 * DEV :]
    for s, part in enumerate(split(beyond, 2)):
        full = res_v[s] + nn(put_v[...], part.astype(BF))
        for g in range(4):
            stage_v[pl.ds(s * 4 + g, DEV, stride=8), :] = full[g * HALF : (g + 1) * HALF, :].T
    pack(out2)
    own2 = send_all(lambda p: out2.at[p], in2, 2)

    gain = 1.0 / math.sqrt(LINES * TILE * STEPS * TM / (2 * DEV * WIDTH))
    filler = jnp.zeros((HALF - SLOT, WIDTH), F32)
    contributions = []
    across = jnp.zeros((SLOT, WIDTH), F32)
    for s in range(2):
        sheet = (sums[s] * gain).astype(BF).astype(F32)
        tall = jnp.concatenate([sheet, filler], axis=0)
        adj_v[s] = jnp.concatenate([tall[:, :HALF].T, tall[:, HALF:].T], axis=0)

        def adjoint(i, state):
            totals, across = list(state[:NNZ]), state[NNZ]
            start = pl.multiple_of(i * CHUNK, CHUNK)
            weights = adj_v[s, pl.ds(start, CHUNK), :]
            for c in range(LANE_COMPS):
                weight = jnp.broadcast_to(weights[:, c : c + 1], (CHUNK, WIDTH))
                for k in range(NNZ):
                    block = kern_v[(s * NNZ + k) * COMPS + c, pl.ds(start, CHUNK), :].astype(F32) * weight
                    totals[k] = totals[k] + jnp.sum(block.reshape(CHUNK // 8, 8, WIDTH), axis=0)
            for c in range(LANE_COMPS, COMPS):
                left = jnp.where(wide_row == s * NNZ + i, sheet[c : c + 1], 0.0).astype(BF)
                across = across + nn(left, kern_v[(s * NNZ + i) * COMPS + c])
            return (*totals, across)

        state = lax.fori_loop(0, NNZ, adjoint, (*[jnp.zeros((8, WIDTH), F32)] * NNZ, across), unroll=2)
        contributions += [jnp.sum(total, axis=0, keepdims=True) for total in state[:NNZ]]
        across = state[NNZ]
    contributions = jnp.concatenate(contributions, axis=0) + across[:PAIRS]
    pieces = split(contributions, 2)
    stack = [piece[:, h * HALF : (h + 1) * HALF] for h in range(2) for piece in pieces]
    stack = jnp.concatenate(stack + [jnp.zeros((HALF - 4 * PAIRS, HALF), F32)], axis=0).astype(BF)
    stage_v[...] = nn(goal_v[...], stack)
    pack(out3)
    own3 = send_all(lambda p: out3.at[p], in3, 3)

    all_arrived(in2, 2, own2)
    unpack(in2)
    for s in range(2):
        for g in range(4):
            wide_v[pl.ds(g * HALF, HALF), pl.ds(s * HALF, HALF)] = (
                stage_v[pl.ds(s * 4 + g, DEV, stride=8), :].T.astype(BF)
            )
    rest = jnp.sum(nn(pick_v[...], wide_v[...]), axis=1, keepdims=True)

    def collect(l, _):
        lanes = pl.ds(pl.multiple_of(l * STEPS, STEPS), STEPS)
        every = nn(wide_v[...], hot_v[:, lanes])
        rank = rank_v[pl.ds(l, 1), :]
        value = jnp.zeros((SLOT, STEPS), F32)
        for r in range(CAP):
            value = value + jnp.where(rank == float(r), every[r * SLOT : (r + 1) * SLOT], 0.0)
        fold_v[pl.ds(pl.multiple_of(l * SLOT, SLOT), SLOT), :] = value
        return 0

    lax.fori_loop(0, LINES, collect, 0, unroll=4)
    onward = onward_v[...]
    late = nn(fold_v[:, WIDTH:].astype(BF), onward) + rest
    soon = nn(fold_v[:, :WIDTH].astype(BF), onward) + late[:, :1]
    scale = 1.0 / math.sqrt(STEPS * TM)
    saves = []
    for j, part in enumerate((soon[:, :HALF], soon[:, HALF:], late[:, :HALF], late[:, HALF:])):
        for l in range(LINES):
            off_v[pl.ds(j * DEV + l, SLOT, stride=LINES), :] = part[l * SLOT : (l + 1) * SLOT] * scale
        save = pltpu.make_async_copy(
            off_v.at[pl.ds(j * DEV, rows)], walk_hbm.at[:, pl.ds(j * HALF, HALF)], save_sem.at[j]
        )
        save.start()
        saves.append(save)

    all_arrived(in3, 3, own3)
    grad = jnp.sum(in3[...].astype(F32), axis=0)
    grad_ref[...] = jnp.concatenate([grad[:4], grad[4:]], axis=1)
    save = pltpu.make_async_copy(grad_ref, grad_hbm, save_sem.at[4])
    save.start()
    for save in saves + [save]:
        save.wait()
    for slot, dst in enumerate((mod_in, in1, in2, in3)):
        all_sent(dst, slot)


def deliver(grad_in, walk_in, grad_out, walk_out):
    walk_out[...] = walk_in[...]
    grad_out[...] = grad_in[...]


def shards(observed, increments, model, kernel, tile_index, station_of, line_length):
    rows = COMPS * LINES
    anywhere = pl.BlockSpec(memory_space=pl.ANY)
    message = pltpu.VMEM((DEV, 8, HALF), BF)
    grad_model, walk = pl.pallas_call(
        body,
        out_shape=(
            jax.ShapeDtypeStruct((4, WIDTH), F32),
            jax.ShapeDtypeStruct((rows, STEPS), F32),
        ),
        in_specs=[anywhere] * 7,
        out_specs=(anywhere, anywhere),
        scratch_shapes=[
            pltpu.VMEM((4, WIDTH), F32),
            pltpu.VMEM((rows, STEPS), F32),
            pltpu.VMEM((rows, STEPS), F32),
            pltpu.VMEM((4, WIDTH), F32),
            pltpu.SMEM((2, NNZ), I32),
            pltpu.VMEM((LINES, STEPS), I32),
            pltpu.SMEM((LINES,), I32),
            pltpu.VMEM((PAIRS * COMPS, WIDTH, WIDTH), BF),
            pltpu.VMEM((WIDTH, LINES * STEPS), BF),
            pltpu.VMEM((CAP * SLOT, LINES * STEPS), BF),
            pltpu.VMEM((LINES, STEPS), F32),
            pltpu.VMEM((4 * DEV, HALF), F32),
            pltpu.VMEM((DEV, CAP * SLOT), BF),
            pltpu.VMEM((CAP * SLOT, DEV), BF),
            pltpu.VMEM((DEV, DEV), BF),
            pltpu.VMEM((DEV, DEV), BF),
            pltpu.VMEM((DEV * 8, HALF), BF),
            pltpu.VMEM((WIDTH, WIDTH), BF),
            pltpu.VMEM((DEV * 8, HALF), F32),
            pltpu.VMEM((WIDTH, CAP * SLOT), F32),
            pltpu.VMEM((2, CAP * SLOT, HALF), F32),
            pltpu.VMEM((DEV, DEV), F32),
            pltpu.VMEM((SLOT, WIDTH), F32),
            pltpu.VMEM((2, SLOT, WIDTH), F32),
            pltpu.VMEM((2, WIDTH, HALF), F32),
            pltpu.VMEM((CAP * SLOT, WIDTH), BF),
            pltpu.VMEM((2, CAP * SLOT, HALF), F32),
            pltpu.VMEM((DEV, STEPS), F32),
            pltpu.VMEM((8, HALF), BF),
            message, message, message, message, message, message, message,
            pltpu.SemaphoreType.DMA((6,)),
            pltpu.SemaphoreType.DMA((5,)),
            pltpu.SemaphoreType.DMA,
            pltpu.SemaphoreType.DMA((4,)),
            pltpu.SemaphoreType.DMA((4,)),
            pltpu.SemaphoreType.DMA((4,)),
        ],
        compiler_params=pltpu.CompilerParams(
            collective_id=0, has_side_effects=True, vmem_limit_bytes=60 * 1024 * 1024
        ),
        name="invert",
    )(
        observed.reshape(rows, STEPS),
        increments.reshape(rows, STEPS),
        model,
        kernel.reshape(PAIRS * COMPS, WIDTH, WIDTH),
        tile_index,
        station_of,
        line_length,
    )
    grad_model, walk = pl.pallas_call(
        deliver,
        out_shape=(
            jax.ShapeDtypeStruct((4, WIDTH), F32),
            jax.ShapeDtypeStruct((rows, STEPS), F32),
        ),
        name="deliver",
    )(grad_model, walk)
    return grad_model, walk.reshape(COMPS, LINES, STEPS)


def solution(mesh):
    in_specs = (
        P(None, "tile", "tm"),
        P(None, "tile", "tm"),
        P(("tm", "tile"), None),
        P(("tm", "tile"), None, None, None, None),
        P(("tm", "tile"), None),
        P("tile", "tm"),
        P("tile"),
    )
    out_specs = (P(("tm", "tile"), None), P(None, "tile", "tm"))
    return jax.shard_map(shards, mesh=mesh, in_specs=in_specs, out_specs=out_specs, check_vma=False)
```
